32 devices in a mesh: dp: 8 (over z, y), tensor: 4 (over x, core).
Axes of the slice: x: 2, y: 2, z: 4, core: 2. Of those that a mesh axis runs over, the one named last changes fastest.
Arguments:
- hidden_in: bfloat16 [4096, 640], P(('dp', 'tensor')), may hold values from -6 to 6
- cotangent: bfloat16 [4096, 640], P(('dp', 'tensor')), may hold values from -6 to 6
- segments: int32 [4096], P('dp'), may hold values from 0 to 3, as said below
- positions: int32 [4096], P('dp'), may hold values from 0 to 508, as said below
- w_query: bfloat16 [2, 640, 1024], P(None, None, 'tensor'), may hold values from -0.25 to 0.25
- w_key: bfloat16 [2, 640, 256], replicated, may hold values from -0.25 to 0.25
- w_value: bfloat16 [2, 640, 256], replicated, may hold values from -0.25 to 0.25
- w_out: bfloat16 [2, 1024, 640], P(None, 'tensor'), may hold values from -0.1875 to 0.1875
- w_gate: bfloat16 [2, 640, 2048], P(None, None, 'tensor'), may hold values from -0.25 to 0.25
- w_up: bfloat16 [2, 640, 2048], P(None, None, 'tensor'), may hold values from -0.25 to 0.25
- w_down: bfloat16 [2, 2048, 640], P(None, 'tensor'), may hold values from -0.125 to 0.125
- norm_gains: float32 [2, 4, 640], replicated, may hold values from 0.5 to 1.5
- qk_gains: float32 [2, 2, 256], replicated, may hold values from 0.5 to 1.5
Outputs:
- output: bfloat16 [4096, 640], P(('dp', 'tensor'))
- grad_input: bfloat16 [4096, 640], P(('dp', 'tensor'))
- grad_w_query: float32 [2, 640, 1024], P(None, 'dp', 'tensor')
- grad_w_key: float32 [2, 640, 256], P(None, 'dp')
- grad_w_value: float32 [2, 640, 256], P(None, 'dp')
- grad_w_out: float32 [2, 1024, 640], P(None, ('tensor', 'dp'))
- grad_w_gate: float32 [2, 640, 2048], P(None, 'dp', 'tensor')
- grad_w_up: float32 [2, 640, 2048], P(None, 'dp', 'tensor')
- grad_w_down: float32 [2, 2048, 640], P(None, ('tensor', 'dp'))
- grad_norm_gains: float32 [2, 4, 640], P(None, None, 'dp')
- grad_qk_gains: float32 [2, 2, 256], P(None, None, 'dp')
The draws below stay inside these ranges and needn't reach their ends.
Inputs may be any that keep to these rules, and one draw needn't show every extreme that they name: `segments`: in each sequence (aligned runs of 512 tokens) the numbers start at 0, never fall, and each of 0 to 3 marks one document of one token or more. `positions`: each token's place in its document, 0 at the document's first token.
All inputs are finite; a program needn't handle non-finite values.
Results may differ from the reference program's by a relative error of at most 0.033.
Values may be sent and summed in bfloat16 or wider, within the bound.
No kernel may reach another device: no remote copies, remote signals or barrier semaphores. Data moves between devices by JAX's collectives and lax.ppermute only.
A program may use at most 128 MiB of HBM per device.

```python
from functools import partial
import jax
import jax.numpy as jnp
from jax import lax

D = 640
HEADS = 4
HD = 256
FF = 2048
WINDOW = 512
SEQ_LEN = 512
NDOC = 4
TOKENS = 4096
HID_SLICE = 512


def doc_layout(key):
    base_key = jax.random.fold_in(key, 7)
    seq_keys = jax.random.split(base_key, TOKENS // SEQ_LEN)
    seq_index = jnp.arange(TOKENS // SEQ_LEN, dtype=jnp.int32)

    def one_sequence(seq_key, which):
        shuffled = jax.random.permutation(seq_key, SEQ_LEN - 1) + 1
        random_cuts = jnp.sort(shuffled[:NDOC - 1]).astype(jnp.int32)
        packed_cuts = jnp.arange(1, NDOC, dtype=jnp.int32)
        cuts = jnp.where(which == 0, packed_cuts, random_cuts).astype(jnp.int32)
        places = jnp.arange(SEQ_LEN, dtype=jnp.int32)
        passed = places[:, None] >= cuts[None, :]
        seg_ids = jnp.sum(passed.astype(jnp.int32), axis=1)
        starts = jnp.max(jnp.where(passed, cuts[None, :], 0), axis=1)
        return (seg_ids.astype(jnp.int32), (places - starts).astype(jnp.int32))
    seg_all, pos_all = jax.vmap(one_sequence)(seq_keys, seq_index)
    return (seg_all.reshape(-1), pos_all.reshape(-1))


def draw_segments(key, part):
    return doc_layout(key)[0]


def draw_positions(key, part):
    return doc_layout(key)[1]


def shard_levels(rng, dims, cuts, low, high):
    def one(dim, parts):
        steps = jax.random.uniform(jax.random.fold_in(jax.random.fold_in(rng, 6), dim), (parts,), jnp.float32, low / len(cuts), high / len(cuts))
        return jnp.repeat(jnp.exp(steps), dims[dim] // parts).reshape((-1,) + (1,) * (len(dims) - dim - 1))

    gain = one(*cuts[0])
    for cut in cuts[1:]:
        gain = gain * one(*cut)
    return gain


def noise(rng, extent, spread, most, cuts=(), held_as=jnp.bfloat16):
    values = spread * jax.random.normal(rng, extent, jnp.float32)
    if cuts:
        values = values * shard_levels(rng, extent, cuts, -0.22, 0.18)
    return jnp.clip(values, -most, most).astype(held_as)


def setup_inputs(seed: int = 0) -> dict:
    keys = jax.random.split(jax.random.key(seed), 14)
    hidden_in = noise(keys[0], (TOKENS, D), 1.0, 6.0, ((0, 32),))
    cotangent = noise(keys[1], (TOKENS, D), 1.0, 6.0, ((0, 32),))
    segments = draw_segments(jax.random.fold_in(keys[13], 71), 0)
    positions = draw_positions(jax.random.fold_in(keys[13], 71), 0)
    w_query = noise(keys[4], (2, D, HEADS * HD), D ** -0.5, 0.25, ((2, 4),))
    w_key = noise(keys[5], (2, D, HD), D ** -0.5, 0.25)
    w_value = noise(keys[6], (2, D, HD), D ** -0.5, 0.25)
    w_out = noise(keys[7], (2, HEADS * HD, D), (HEADS * HD) ** -0.5, 0.1875, ((1, 4),))
    w_gate = noise(keys[8], (2, D, FF), D ** -0.5, 0.25, ((2, 4),))
    w_up = noise(keys[9], (2, D, FF), D ** -0.5, 0.25, ((2, 4),))
    w_down = noise(keys[10], (2, FF, D), FF ** -0.5, 0.125, ((1, 4),))
    norm_gains = jnp.clip(1.0 + 0.1 * jax.random.normal(keys[11], (2, 4, D), jnp.float32), 0.5, 1.5)
    qk_gains = jnp.clip(1.0 + 0.1 * jax.random.normal(keys[12], (2, 2, HD), jnp.float32), 0.5, 1.5)
    return {"hidden_in": hidden_in, "cotangent": cotangent, "segments": segments, "positions": positions, "w_query": w_query, "w_key": w_key, "w_value": w_value, "w_out": w_out, "w_gate": w_gate, "w_up": w_up, "w_down": w_down, "norm_gains": norm_gains, "qk_gains": qk_gains}


@jax.custom_vjp
def low(v):
    return lax.optimization_barrier(v.astype(jnp.bfloat16)).astype(jnp.float32)

@jax.custom_vjp
def low_back(v):
    return v

def low_keep(v):
    return (low(v), None)

def low_pass(kept, grad):
    return (grad,)

def back_keep(v):
    return (v, None)

def back_low(kept, grad):
    return (low(grad),)
low.defvjp(low_keep, low_pass)
low_back.defvjp(back_keep, back_low)
epsilon = 1e-06
score_scale = 0.0625
masked_fill = -1e+30
thetas = (10000.0, 1000000.0)

def matmul(left, right):
    return jnp.dot(left, right, precision=lax.Precision.HIGHEST, preferred_element_type=jnp.float32)

def rms_scale(vector, gain_row):
    return vector * lax.rsqrt(lax.optimization_barrier(jnp.mean(vector * vector, axis=-1, keepdims=True)) + epsilon) * gain_row

def angles(place, width, theta):
    half_width = width // 2
    frequency = theta ** (-(2.0 * jnp.arange(half_width, dtype=jnp.float32)) / width)
    phases = place.astype(jnp.float32)[:, None] * frequency[None, :]
    return (jnp.cos(phases), jnp.sin(phases))

def rotate(vector, cosine, sine):
    half_width = vector.shape[-1] // 2
    first_half = vector[:, :half_width]
    second_half = vector[:, half_width:]
    return jnp.concatenate([first_half * cosine - second_half * sine, second_half * cosine + first_half * sine], axis=-1)

def allowed_mask(seg_piece, window):
    length = seg_piece.shape[0]
    rows_iota = lax.broadcasted_iota(jnp.int32, (length, length), 0)
    cols_iota = lax.broadcasted_iota(jnp.int32, (length, length), 1)
    return (seg_piece[:, None] == seg_piece[None, :]) & (cols_iota <= rows_iota) & (rows_iota - cols_iota < window)

def ref_attend(pieces, window):
    queries, key_rows, values, seg_piece = pieces
    scores = low_back(matmul(queries, key_rows.T) * score_scale)
    allowed = allowed_mask(seg_piece, window)
    masked = jnp.where(allowed, scores, masked_fill)
    row_max = lax.optimization_barrier(jnp.max(masked, axis=-1, keepdims=True))
    expo = jnp.where(allowed, jnp.exp(masked - row_max), 0.0)
    probability = low(expo / lax.optimization_barrier(jnp.sum(expo, axis=-1, keepdims=True)))
    return matmul(probability, values)

def ref_layer(stream, params, seg_rows, pos_rows, theta, window):
    w_q, w_k, w_v, w_o, w_g, w_u, w_d, gains, qk_gain = params
    cosine, sine = angles(pos_rows, HD, theta)
    attend_fn = jax.checkpoint(partial(ref_attend, window=window))
    normed = low(rms_scale(stream, gains[0]))
    attn_sum = jnp.zeros_like(stream)
    for branch in range(HEADS):
        head_in = low_back(normed)
        query_raw = low_back(matmul(head_in, w_q[:, branch * HD:(branch + 1) * HD]))
        key_raw = low_back(matmul(head_in, w_k))
        values = low_back(low(matmul(head_in, w_v)))
        queries = low_back(low(rotate(rms_scale(query_raw, qk_gain[0]), cosine, sine)))
        key_rows = low_back(low(rotate(rms_scale(key_raw, qk_gain[1]), cosine, sine)))
        attended = lax.map(attend_fn, (queries.reshape(-1, SEQ_LEN, HD), key_rows.reshape(-1, SEQ_LEN, HD), values.reshape(-1, SEQ_LEN, HD), seg_rows.reshape(-1, SEQ_LEN)))
        attended = low_back(low(attended.reshape(-1, HD)))
        attn_sum = attn_sum + low(matmul(attended, w_o[branch * HD:(branch + 1) * HD]))
    attn_sum = low_back(attn_sum)
    middle = stream + rms_scale(attn_sum, gains[1])
    normed_mlp = low(rms_scale(middle, gains[2]))
    mlp_sum = jnp.zeros_like(stream)
    for branch in range(HEADS):
        slice_in = low_back(normed_mlp)
        lo_col = branch * HID_SLICE
        gate_pre = low_back(matmul(slice_in, w_g[:, lo_col:lo_col + HID_SLICE]))
        up_pre = low_back(matmul(slice_in, w_u[:, lo_col:lo_col + HID_SLICE]))
        hidden = low(jax.nn.gelu(gate_pre, approximate=True) * up_pre)
        mlp_sum = mlp_sum + low(matmul(hidden, w_d[lo_col:lo_col + HID_SLICE]))
    mlp_sum = low_back(mlp_sum)
    return middle + rms_scale(mlp_sum, gains[3])

def model_forward(stream, params, seg_rows, pos_rows):
    windows = (WINDOW, SEQ_LEN)
    for layer_idx in range(2):
        layer_params = tuple((param[layer_idx] for param in params))
        stream = ref_layer(stream, layer_params, seg_rows, pos_rows, thetas[layer_idx], windows[layer_idx])
    return stream

def reference(hidden_in, cotangent, segments, positions, w_query, w_key, w_value, w_out, w_gate, w_up, w_down, norm_gains, qk_gains):
    params = tuple((weight.astype(jnp.float32) for weight in (w_query, w_key, w_value, w_out, w_gate, w_up, w_down, norm_gains, qk_gains)))
    seq_count = TOKENS // SEQ_LEN
    group_seqs = 8 if seq_count % 8 == 0 else 1
    group_count = seq_count // group_seqs
    group_rows = group_seqs * SEQ_LEN
    streams = hidden_in.astype(jnp.float32).reshape(group_count, group_rows, D)
    grads_in = cotangent.astype(jnp.float32).reshape(group_count, group_rows, D)
    seg_groups = segments.astype(jnp.int32).reshape(group_count, group_rows)
    pos_groups = positions.astype(jnp.int32).reshape(group_count, group_rows)

    def step_group(carry, pieces):
        stream_in, grad_in, seg_rows, pos_rows = pieces

        def forward(stream_arg, param_arg):
            return model_forward(stream_arg, param_arg, seg_rows, pos_rows)
        result, pullback = jax.vjp(forward, stream_in, params)
        grad_stream, grad_params = pullback(grad_in)
        carry = jax.tree.map(lambda acc_sum, addend: acc_sum + addend, carry, grad_params)
        return (carry, (result, grad_stream))
    init_grads = jax.tree.map(jnp.zeros_like, params)
    sums, (results, grad_streams) = lax.scan(step_group, init_grads, (streams, grads_in, seg_groups, pos_groups))
    output = results.reshape(TOKENS, D).astype(jnp.bfloat16)
    grad_input = grad_streams.reshape(TOKENS, D).astype(jnp.bfloat16)
    return (output, grad_input, sums[0], sums[1], sums[2], sums[3], sums[4], sums[5], sums[6], sums[7], sums[8])
```

```python
import jax
import jax.numpy as jnp
from jax import lax
from jax.sharding import PartitionSpec as P

WINDOW = 512
SEQ_LEN = 512
LANES = 128
GAIN_ROWS = 16

epsilon = 1e-06
score_scale = 0.0625
masked_fill = -1e30
thetas = (10000.0, 1000000.0)


def product(left, right):
    return jnp.dot(left, right, preferred_element_type=jnp.float32)


def product_left(left, right):
    return lax.dot_general(
        left, right, (((0,), (0,)), ((), ())), preferred_element_type=jnp.float32
    )


def product_right(left, right):
    return lax.dot_general(
        left, right, (((1,), (1,)), ((), ())), preferred_element_type=jnp.float32
    )


def rms_scale(vector, gain_row):
    return (
        vector * lax.rsqrt(jnp.mean(vector * vector, axis=-1, keepdims=True) + epsilon) * gain_row
    )


def angles(place, width, theta):
    half_width = width // 2
    frequency = theta ** (-(2.0 * jnp.arange(half_width, dtype=jnp.float32)) / width)
    phases = place.astype(jnp.float32)[:, None] * frequency[None, :]
    return (jnp.cos(phases), jnp.sin(phases))


def rotate(vector, cosine, sine):
    half_width = vector.shape[-1] // 2
    first_half = vector[:, :half_width]
    second_half = vector[:, half_width:]
    return jnp.concatenate(
        [first_half * cosine - second_half * sine, second_half * cosine + first_half * sine],
        axis=-1,
    )


def allowed_mask(seg_piece, place, window):
    return (
        (seg_piece[:, None] == seg_piece[None, :])
        & (place[None, :] <= place[:, None])
        & (place[:, None] - place[None, :] < window)
    )


def swap(array, axis, bit):
    size = lax.axis_size(axis)
    return lax.ppermute(array, axis, [(i, i ^ bit) for i in range(size)])


def relative_order(array, quarter):
    parts = array.reshape((4, -1) + array.shape[1:])
    return jnp.concatenate(
        [lax.dynamic_index_in_dim(parts, quarter ^ bit, 0, False) for bit in (0, 2, 1, 3)]
    )


def own_rows(partial):
    half = partial.shape[0] // 2
    low = partial.astype(jnp.bfloat16)
    pair = (
        low[:half].astype(jnp.float32) + swap(low[half:], "tensor", 1).astype(jnp.float32)
    ).astype(jnp.bfloat16)
    other = swap(pair, "tensor", 2)
    quarter = half // 2
    flipped = jnp.concatenate([other[quarter:], other[:quarter]])
    return pair.astype(jnp.float32) + flipped.astype(jnp.float32)


def all_rows(own):
    return jnp.concatenate([own, swap(own, "tensor", 1)])


def two_quarters(array):
    return jnp.concatenate([array, swap(array, "tensor", 2)])


def norm_back(vector, gain_row, grad_out):
    unused, pullback = jax.vjp(rms_scale, vector, gain_row)
    return pullback(grad_out)


def attend_forward(queries, key_rows, values, allowed):
    scores = product_right(queries, key_rows) * score_scale
    masked = jnp.where(allowed, scores, masked_fill)
    row_max = jnp.max(masked, axis=-1, keepdims=True)
    expo = jnp.where(allowed, jnp.exp(masked - row_max), 0.0)
    row_sum = jnp.sum(expo, axis=-1, keepdims=True)
    probability = (expo / row_sum).astype(jnp.bfloat16)
    attended = product(probability, values)
    return (attended, row_max + jnp.log(row_sum))


def attend_backward(queries, key_rows, values, allowed, row_lse, grad_out):
    scores = product_right(queries, key_rows) * score_scale
    probability = jnp.where(allowed, jnp.exp(scores - row_lse), 0.0)
    prob_low = probability.astype(jnp.bfloat16)
    grad_values = product_left(prob_low, grad_out).astype(jnp.bfloat16)
    grad_prob = product_right(grad_out, values)
    inner_sum = jnp.sum(probability * grad_prob, axis=-1, keepdims=True)
    grad_scores = (probability * (grad_prob - inner_sum)).astype(jnp.bfloat16)
    grad_queries = (product(grad_scores, key_rows) * score_scale).astype(jnp.bfloat16)
    grad_keys = (product_left(grad_scores, queries) * score_scale).astype(jnp.bfloat16)
    return (grad_queries, grad_keys, grad_values)


def gated_unit(gate_in, up_in):
    return jax.nn.gelu(gate_in, approximate=True) * up_in


def layer_forward(stream, weights, allowed, cosine, sine):
    w_query, w_key, w_value, w_out, w_gate, w_up, w_down, gains, qk_gain = weights
    normed = all_rows(rms_scale(stream, gains[0]).astype(jnp.bfloat16))
    query_raw = product(normed, w_query)
    key_raw = product(normed, w_key)
    values = product(normed, w_value).astype(jnp.bfloat16)
    queries = rotate(rms_scale(query_raw, qk_gain[0]), cosine, sine).astype(jnp.bfloat16)
    key_rows = rotate(rms_scale(key_raw, qk_gain[1]), cosine, sine).astype(jnp.bfloat16)
    attended, row_lse = attend_forward(queries, key_rows, values, allowed)
    attn_low = attended.astype(jnp.bfloat16)
    attn_sum = own_rows(product(attn_low, w_out))
    middle = stream + rms_scale(attn_sum, gains[1])
    normed_mlp = all_rows(rms_scale(middle, gains[2]).astype(jnp.bfloat16))
    gate_pre = product(normed_mlp, w_gate)
    up_pre = product(normed_mlp, w_up)
    hidden = gated_unit(gate_pre, up_pre).astype(jnp.bfloat16)
    mlp_sum = own_rows(product(hidden, w_down))
    result = middle + rms_scale(mlp_sum, gains[3])
    saved = (
        stream,
        normed,
        query_raw,
        key_raw,
        queries,
        key_rows,
        values,
        row_lse,
        attn_low,
        attn_sum,
        middle,
        normed_mlp,
        gate_pre,
        up_pre,
        hidden,
        mlp_sum,
    )
    return (result, saved)


def layer_backward(grad_stream, weights, saved, allowed, cosine, sine):
    w_query, w_key, w_value, w_out, w_gate, w_up, w_down, gains, qk_gain = weights
    (
        stream,
        normed,
        query_raw,
        key_raw,
        queries,
        key_rows,
        values,
        row_lse,
        attn_low,
        attn_sum,
        middle,
        normed_mlp,
        gate_pre,
        up_pre,
        hidden,
        mlp_sum,
    ) = saved
    grad_mlp, grad_gain3 = norm_back(mlp_sum, gains[3], grad_stream)
    mlp_low = all_rows(grad_mlp.astype(jnp.bfloat16))
    grad_hidden = product_right(mlp_low, w_down)
    unused, gate_pull = jax.vjp(gated_unit, gate_pre, up_pre)
    grad_gate, grad_up = gate_pull(grad_hidden)
    gate_low = grad_gate.astype(jnp.bfloat16)
    up_low = grad_up.astype(jnp.bfloat16)
    grad_normed_mlp = own_rows(product_right(gate_low, w_gate) + product_right(up_low, w_up))
    grad_w_down = product_left(hidden, mlp_low)
    grad_w_gate = product_left(normed_mlp, gate_low)
    grad_w_up = product_left(normed_mlp, up_low)
    grad_middle_norm, grad_gain2 = norm_back(middle, gains[2], grad_normed_mlp)
    grad_middle = grad_stream + grad_middle_norm
    grad_attn, grad_gain1 = norm_back(attn_sum, gains[1], grad_middle)
    attn_grad_low = all_rows(grad_attn.astype(jnp.bfloat16))
    grad_attended = product_right(attn_grad_low, w_out).astype(jnp.bfloat16)
    grad_queries, grad_keys, grad_values = attend_backward(
        queries, key_rows, values, allowed, row_lse, grad_attended
    )

    def qk_chain(raw_rows, gain_row):
        return rotate(rms_scale(raw_rows, gain_row), cosine, sine)

    unused, query_pull = jax.vjp(qk_chain, query_raw, qk_gain[0])
    grad_query_raw, grad_query_gain = query_pull(grad_queries.astype(jnp.float32))
    unused, key_pull = jax.vjp(qk_chain, key_raw, qk_gain[1])
    grad_key_raw, grad_key_gain = key_pull(grad_keys.astype(jnp.float32))
    query_low = grad_query_raw.astype(jnp.bfloat16)
    key_low = grad_key_raw.astype(jnp.bfloat16)
    grad_normed = own_rows(
        product_right(query_low, w_query)
        + product_right(key_low, w_key)
        + product_right(grad_values, w_value)
    )
    grad_w_out = product_left(attn_low, attn_grad_low)
    grad_w_query = product_left(normed, query_low)
    grad_w_key = product_left(normed, key_low)
    grad_w_value = product_left(normed, grad_values)
    grad_stream_norm, grad_gain0 = norm_back(stream, gains[0], grad_normed)
    grad_input = grad_middle + grad_stream_norm
    mlp_grads = (grad_w_gate, grad_w_up, grad_w_down)
    attn_grads = (grad_w_query, grad_w_out, grad_w_key, grad_w_value)
    norm_gain_grads = jnp.stack([grad_gain0, grad_gain1, grad_gain2, grad_gain3])
    qk_gain_grads = jnp.stack([grad_query_gain, grad_key_gain])
    return (grad_input, mlp_grads, attn_grads, norm_gain_grads, qk_gain_grads)


def packed(array, pieces):
    rows, columns = array.shape
    low = array.astype(jnp.bfloat16).reshape(pieces, rows // pieces, columns // LANES, LANES)
    return low.transpose(0, 2, 1, 3).reshape(pieces, -1, LANES)


def unpacked(rows, columns):
    count = columns // LANES
    return rows.reshape(count, -1, LANES).transpose(1, 0, 2).reshape(-1, columns)


def packed_gains(norm_gain_grads, qk_gain_grads, pieces):
    def spread(array):
        count, columns = array.shape
        block = array.reshape(count, pieces, columns // pieces).transpose(1, 0, 2)
        return jnp.pad(block, ((0, 0), (0, 0), (0, LANES - columns // pieces)))

    block = jnp.concatenate([spread(norm_gain_grads * 0.5), spread(qk_gain_grads)], axis=1)
    return jnp.pad(block, ((0, 0), (0, GAIN_ROWS - block.shape[1]), (0, 0))).astype(jnp.bfloat16)


def halved(blocks):
    me = lax.axis_index("dp")
    bit = 1
    while blocks.shape[0] > 1:
        low = blocks.astype(jnp.bfloat16).reshape((-1, 2) + blocks.shape[1:])
        side = jnp.bitwise_and(me // bit, 1)
        kept = lax.dynamic_index_in_dim(low, side, 1, False)
        sent = lax.dynamic_index_in_dim(low, 1 - side, 1, False)
        blocks = kept.astype(jnp.float32) + swap(sent, "dp", bit).astype(jnp.float32)
        bit *= 2
    return blocks[0]


def over_tensor(rows):
    for bit in (1, 2):
        low = rows.astype(jnp.bfloat16)
        rows = low.astype(jnp.float32) + swap(low, "tensor", bit).astype(jnp.float32)
    return rows


def local(
    hidden_in,
    cotangent,
    segments,
    positions,
    w_query,
    w_key,
    w_value,
    w_out,
    w_gate,
    w_up,
    w_down,
    norm_gains,
    qk_gains,
):
    head_width = w_key.shape[2]
    windows = (WINDOW, SEQ_LEN)
    pieces = lax.axis_size("dp")
    quarter = lax.axis_index("tensor")
    seg_rows = relative_order(segments, quarter)
    pos_rows = relative_order(positions, quarter)
    places = relative_order(jnp.arange(SEQ_LEN, dtype=jnp.int32), quarter)
    stream = two_quarters(hidden_in).astype(jnp.float32)
    saved_all = []
    tables = []
    layer_weights = []
    for layer_idx in range(2):
        cosine, sine = angles(pos_rows, head_width, thetas[layer_idx])
        allowed = allowed_mask(seg_rows, places, windows[layer_idx])
        weights = (
            w_query[layer_idx],
            w_key[layer_idx],
            w_value[layer_idx],
            w_out[layer_idx],
            w_gate[layer_idx],
            w_up[layer_idx],
            w_down[layer_idx],
            norm_gains[layer_idx],
            qk_gains[layer_idx],
        )
        stream, saved = layer_forward(stream, weights, allowed, cosine, sine)
        saved_all.append(saved)
        tables.append((allowed, cosine, sine))
        layer_weights.append(weights)
    own = hidden_in.shape[0]
    output = stream[:own].astype(jnp.bfloat16)
    grad_stream = two_quarters(cotangent).astype(jnp.float32)

    grad_stream, mlp1, attn1, norm1, qk1 = layer_backward(
        grad_stream, layer_weights[1], saved_all[1], *tables[1]
    )
    whole = jnp.concatenate([packed(g, pieces) for g in mlp1 + attn1], axis=1)
    rows1 = lax.psum_scatter(
        whole.reshape(-1, LANES), "dp", scatter_dimension=0, tiled=True
    ).astype(jnp.float32)

    grad_stream, mlp0, attn0, norm0, qk0 = layer_backward(
        grad_stream, layer_weights[0], saved_all[0], *tables[0]
    )
    mlp_rows0 = halved(jnp.concatenate([packed(g, pieces) for g in mlp0], axis=1))
    attn_rows0 = halved(jnp.concatenate([packed(g, pieces) for g in attn0], axis=1))
    gain_rows = halved(
        jnp.concatenate(
            [packed_gains(norm0, qk0, pieces), packed_gains(norm1, qk1, pieces)], axis=1
        )
    )
    rows0 = jnp.concatenate([mlp_rows0, attn_rows0])

    sizes = [w.shape[0] * w.shape[1] // (LANES * pieces) for w in mlp1 + attn1]
    columns = [w.shape[1] for w in mlp1 + attn1]
    starts = [sum(sizes[:i]) for i in range(len(sizes) + 1)]
    shared = over_tensor(
        jnp.concatenate([rows1[starts[5] :], rows0[starts[5] :], gain_rows])
    )
    both = sizes[5] + sizes[6]

    def outs(member):
        if member < 5:
            picks = [rows[starts[member] : starts[member + 1]] for rows in (rows0, rows1)]
        else:
            offset = starts[member] - starts[5]
            picks = [
                shared[base + offset : base + offset + sizes[member]] for base in (both, 0)
            ]
        return jnp.stack([unpacked(rows, columns[member]) for rows in picks])

    gains = shared[2 * both :].reshape(2, GAIN_ROWS, LANES)
    grad_norm_gains = gains[:, :4, : norm_gains.shape[2] // pieces]
    grad_qk_gains = gains[:, 4:6, : qk_gains.shape[2] // pieces]
    grad_input = grad_stream[:own].astype(jnp.bfloat16)
    return (
        output,
        grad_input,
        outs(3),
        outs(5),
        outs(6),
        outs(4),
        outs(0),
        outs(1),
        outs(2),
        grad_norm_gains,
        grad_qk_gains,
    )


def solution(mesh):
    return jax.shard_map(
        local,
        mesh=mesh,
        in_specs=(
            P(("dp", "tensor"), None),
            P(("dp", "tensor"), None),
            P("dp"),
            P("dp"),
            P(None, None, "tensor"),
            P(),
            P(),
            P(None, "tensor", None),
            P(None, None, "tensor"),
            P(None, None, "tensor"),
            P(None, "tensor", None),
            P(),
            P(),
        ),
        out_specs=(
            P(("dp", "tensor"), None),
            P(("dp", "tensor"), None),
            P(None, "dp", "tensor"),
            P(None, "dp", None),
            P(None, "dp", None),
            P(None, ("tensor", "dp"), None),
            P(None, "dp", "tensor"),
            P(None, "dp", "tensor"),
            P(None, ("tensor", "dp"), None),
            P(None, None, "dp"),
            P(None, None, "dp"),
        ),
        check_vma=False,
    )
```

```python
import jax
import jax.numpy as jnp
from jax import lax
from jax.experimental import pallas as pl
from jax.experimental.pallas import tpu as pltpu
from jax.sharding import PartitionSpec as P

WINDOW = 512
SEQ_LEN = 512
LANES = 128

epsilon = 1e-06
score_scale = 0.0625
masked_fill = -1e30
thetas = (10000.0, 1000000.0)
gelu_slope = 0.7978845608028654
gelu_cubic = 0.044715

F32 = jnp.float32
BF16 = jnp.bfloat16


def product(left, right):
    return jnp.dot(left, right, preferred_element_type=F32)


def product_left(left, right):
    return lax.dot_general(left, right, (((0,), (0,)), ((), ())), preferred_element_type=F32)


def product_right(left, right):
    return lax.dot_general(left, right, (((1,), (1,)), ((), ())), preferred_element_type=F32)


def angles(place, width, theta):
    half_width = width // 2
    frequency = theta ** (-(2.0 * jnp.arange(half_width, dtype=F32)) / width)
    phases = place.astype(F32)[:, None] * frequency[None, :]
    return (jnp.cos(phases), jnp.sin(phases))


def swap(array, axis, bit):
    size = lax.axis_size(axis)
    return lax.ppermute(array, axis, [(i, i ^ bit) for i in range(size)])


def relative_order(array, quarter):
    parts = array.reshape((4, -1) + array.shape[1:])
    return jnp.concatenate(
        [lax.dynamic_index_in_dim(parts, quarter ^ bit, 0, False) for bit in (0, 2, 1, 3)]
    )


def two_quarters(array):
    return jnp.concatenate([array, swap(array, "tensor", 2)])


def summed_pair(kept, sent):
    pair = (kept.astype(F32) + swap(sent, "tensor", 1).astype(F32)).astype(BF16)
    return (pair, swap(pair, "tensor", 2))


def kernel_call(body, outs, args, layers=None, flops=0):
    layers = layers or {}

    def spec(place, arg):
        if place in layers:
            rest = arg.shape[1:]
            fixed = (layers[place],) + (0,) * len(rest)
            return pl.BlockSpec((1,) + rest, lambda i, fixed=fixed: fixed)
        if arg.shape == (1,):
            return pl.BlockSpec(memory_space=pltpu.SMEM)
        return pl.BlockSpec(arg.shape, lambda i, n=arg.ndim: (0,) * n)

    moved = sum(a.size * a.dtype.itemsize for a in args)
    return pl.pallas_call(
        body,
        grid=(1,),
        in_specs=[spec(place, arg) for place, arg in enumerate(args)],
        out_specs=[pl.BlockSpec(o.shape, lambda i, n=len(o.shape): (0,) * n) for o in outs],
        out_shape=list(outs),
        compiler_params=pltpu.CompilerParams(vmem_limit_bytes=40 << 20),
        cost_estimate=pl.CostEstimate(flops=flops, transcendentals=0, bytes_accessed=moved),
    )(*args)


def shape(rows, columns, dtype):
    return jax.ShapeDtypeStruct((rows, columns), dtype)


def inverse_rms(vector):
    return lax.rsqrt(jnp.mean(vector * vector, axis=-1, keepdims=True) + epsilon)


def norm_forward(vector, gain_row):
    return vector * inverse_rms(vector) * gain_row


def norm_back(vector, gain_row, grad_out):
    scale = inverse_rms(vector)
    scaled = grad_out * gain_row
    inner = jnp.mean(scaled * vector, axis=-1, keepdims=True)
    grad = scale * scaled - vector * (scale * scale * scale * inner)
    grad_gain = jnp.sum(grad_out * (vector * scale), axis=0, keepdims=True)
    return (grad, grad_gain)


def rotate(vector, cosine, sine):
    half_width = vector.shape[-1] // 2
    first_half = vector[:, :half_width]
    second_half = vector[:, half_width:]
    return jnp.concatenate(
        [first_half * cosine - second_half * sine, second_half * cosine + first_half * sine],
        axis=-1,
    )


def total(pair_ref, other_ref):
    quarter = pair_ref.shape[0] // 2
    other = jnp.concatenate([other_ref[quarter:, :], other_ref[:quarter, :]], axis=0)
    return pair_ref[...].astype(F32) + other.astype(F32)


def first_norm(stream, gains, layer):
    def body(stream_ref, gains_ref, normed_ref):
        normed_ref[...] = norm_forward(
            stream_ref[...].astype(F32), gains_ref[0, 0:1, :]
        ).astype(BF16)

    return kernel_call(body, [shape(*stream.shape, BF16)], (stream, gains), {1: layer})[0]


def after_attention(pair, other, stream, gains, layer):
    def body(pair_ref, other_ref, stream_ref, gains_ref, sum_ref, middle_ref, normed_ref):
        attn_sum = total(pair_ref, other_ref)
        middle = stream_ref[...].astype(F32) + norm_forward(attn_sum, gains_ref[0, 1:2, :])
        sum_ref[...] = attn_sum
        middle_ref[...] = middle
        normed_ref[...] = norm_forward(middle, gains_ref[0, 2:3, :]).astype(BF16)

    size = pair.shape
    return kernel_call(
        body,
        [shape(*size, F32), shape(*size, F32), shape(*size, BF16)],
        (pair, other, stream, gains),
        {3: layer},
    )


def between_layers(pair, other, middle, gains, layer):
    def body(pair_ref, other_ref, middle_ref, gains_ref, next_ref, sum_ref, result_ref, low_ref):
        mlp_sum = total(pair_ref, other_ref)
        result = middle_ref[...] + norm_forward(mlp_sum, gains_ref[0, 3:4, :])
        sum_ref[...] = mlp_sum
        result_ref[...] = result
        low_ref[...] = norm_forward(result, next_ref[0, 0:1, :]).astype(BF16)

    size = pair.shape
    return kernel_call(
        body,
        [shape(*size, F32), shape(*size, F32), shape(*size, BF16)],
        (pair, other, middle, gains, gains),
        {3: layer, 4: layer + 1},
    )


def turn_around(pair, other, middle, cotangent, gains, layer):
    def body(pair_ref, other_ref, middle_ref, grad_ref, gains_ref, out_ref, low_ref, gain_ref):
        mlp_sum = total(pair_ref, other_ref)
        gain_row = gains_ref[0, 3:4, :]
        own = out_ref.shape[0]
        result = middle_ref[:own, :] + norm_forward(mlp_sum[:own, :], gain_row)
        out_ref[...] = result.astype(BF16)
        grad, grad_gain = norm_back(mlp_sum, gain_row, grad_ref[...].astype(F32))
        low_ref[...] = grad.astype(BF16)
        gain_ref[...] = grad_gain

    rows, columns = pair.shape
    return kernel_call(
        body,
        [shape(rows // 2, columns, BF16), shape(rows, columns, BF16), shape(1, columns, F32)],
        (pair, other, middle, cotangent, gains),
        {4: layer},
    )


def back_to_attention(pair, other, middle, attn_sum, grad_stream, gains, layer):
    def body(
        pair_ref, other_ref, middle_ref, attn_ref, grad_ref, gains_ref,
        grad_middle_ref, low_ref, gain1_ref, gain2_ref,
    ):
        grad_normed = total(pair_ref, other_ref)
        step, gain2_ref[...] = norm_back(middle_ref[...], gains_ref[0, 2:3, :], grad_normed)
        grad_middle = grad_ref[...].astype(F32) + step
        grad_middle_ref[...] = grad_middle
        grad_attn, gain1_ref[...] = norm_back(attn_ref[...], gains_ref[0, 1:2, :], grad_middle)
        low_ref[...] = grad_attn.astype(BF16)

    rows, columns = pair.shape
    return kernel_call(
        body,
        [shape(rows, columns, F32), shape(rows, columns, BF16)] + [shape(1, columns, F32)] * 2,
        (pair, other, middle, attn_sum, grad_stream, gains),
        {5: layer},
    )


def back_between(pair, other, stream, grad_middle, mlp_sum, gains, layer):
    def body(
        pair_ref, other_ref, stream_ref, grad_ref, mlp_ref, gains_ref, below_ref,
        grad_stream_ref, low_ref, gain0_ref, gain3_ref,
    ):
        grad_normed = total(pair_ref, other_ref)
        step, gain0_ref[...] = norm_back(stream_ref[...], gains_ref[0, 0:1, :], grad_normed)
        grad_stream = grad_ref[...] + step
        grad_stream_ref[...] = grad_stream
        grad_mlp, gain3_ref[...] = norm_back(mlp_ref[...], below_ref[0, 3:4, :], grad_stream)
        low_ref[...] = grad_mlp.astype(BF16)

    rows, columns = pair.shape
    return kernel_call(
        body,
        [shape(rows, columns, F32), shape(rows, columns, BF16)] + [shape(1, columns, F32)] * 2,
        (pair, other, stream, grad_middle, mlp_sum, gains, gains),
        {5: layer, 6: layer - 1},
    )


def back_to_input(pair, other, stream, grad_middle, gains, layer):
    def body(pair_ref, other_ref, stream_ref, grad_ref, gains_ref, out_ref, gain0_ref):
        grad_normed = total(pair_ref, other_ref)
        step, gain0_ref[...] = norm_back(
            stream_ref[...].astype(F32), gains_ref[0, 0:1, :], grad_normed
        )
        own = out_ref.shape[0]
        out_ref[...] = (grad_ref[:own, :] + step[:own, :]).astype(BF16)

    rows, columns = pair.shape
    return kernel_call(
        body,
        [shape(rows // 2, columns, BF16), shape(1, columns, F32)],
        (pair, other, stream, grad_middle, gains),
        {4: layer},
    )


def allowed_rows(down_ref, across_ref, start, count, window):
    seg_down = down_ref[start : start + count, 0:1]
    place_down = down_ref[start : start + count, 1:2]
    seg_across = across_ref[0:1, :]
    place_across = across_ref[1:2, :]
    allowed = (seg_down == seg_across) & (place_across <= place_down)
    if window < SEQ_LEN:
        allowed = allowed & (place_down - place_across < window)
    return allowed


def attention(own, received, weights, tables, layer, window):
    w_query, w_key, w_value, w_out, qk_gains = weights
    cosine, sine, down, across = tables
    half = own.shape[0]
    length = 2 * half
    head_width = w_key.shape[2]

    def body(
        own_ref, received_ref, wq_ref, wk_ref, wv_ref, wo_ref, gain_ref,
        cos_ref, sin_ref, down_ref, across_ref,
        kept_ref, sent_ref, qraw_ref, kraw_ref, q_ref, k_ref, v_ref, attended_ref, lse_ref,
    ):
        for part, source in ((0, own_ref), (1, received_ref)):
            rows = slice(part * half, (part + 1) * half)
            normed = source[...]
            cos_rows, sin_rows = cos_ref[rows, :], sin_ref[rows, :]
            key_raw = product(normed, wk_ref[0])
            kraw_ref[rows, :] = key_raw
            k_ref[rows, :] = rotate(
                norm_forward(key_raw, gain_ref[0, 1:2, :]), cos_rows, sin_rows
            ).astype(BF16)
            v_ref[rows, :] = product(normed, wv_ref[0]).astype(BF16)
            query_raw = product(normed, wq_ref[0])
            qraw_ref[rows, :] = query_raw
            q_ref[rows, :] = rotate(
                norm_forward(query_raw, gain_ref[0, 0:1, :]), cos_rows, sin_rows
            ).astype(BF16)
        for part, target in ((1, sent_ref), (0, kept_ref)):
            rows = slice(part * half, (part + 1) * half)
            scores = product_right(q_ref[rows, :], k_ref[...]) * score_scale
            allowed = allowed_rows(down_ref, across_ref, part * half, half, window)
            masked = jnp.where(allowed, scores, masked_fill)
            row_max = jnp.max(masked, axis=-1, keepdims=True)
            expo = jnp.where(allowed, jnp.exp(masked - row_max), 0.0)
            row_sum = jnp.sum(expo, axis=-1, keepdims=True)
            probability = (expo * (1.0 / row_sum)).astype(BF16)
            lse_ref[rows, :] = row_max + jnp.log(row_sum)
            attended = product(probability, v_ref[...]).astype(BF16)
            attended_ref[rows, :] = attended
            target[...] = product(attended, wo_ref[0]).astype(BF16)

    width = own.shape[1]
    return kernel_call(
        body,
        [shape(half, width, BF16)] * 2
        + [shape(length, head_width, F32)] * 2
        + [shape(length, head_width, BF16)] * 4
        + [shape(length, 1, F32)],
        (own, received, w_query, w_key, w_value, w_out, qk_gains, cosine, sine, down, across),
        {place: layer for place in (2, 3, 4, 5, 6)},
        flops=1_000_000_000,
    )


def feed_forward(own, received, weights, layer):
    half, width = own.shape
    w_gate, w_up, w_down = weights
    hidden_width = w_gate.shape[2]
    length = 2 * half

    def body(own_ref, received_ref, wg_ref, wu_ref, wd_ref, kept_ref, sent_ref, g_ref, u_ref, h_ref):
        for part, source, target in ((1, received_ref, sent_ref), (0, own_ref, kept_ref)):
            rows = slice(part * half, (part + 1) * half)
            normed = source[...]
            gate = product(normed, wg_ref[0])
            up = product(normed, wu_ref[0])
            g_ref[rows, :] = gate
            u_ref[rows, :] = up
            bend = jnp.tanh(gelu_slope * (gate + gelu_cubic * (gate * gate * gate)))
            hidden = (gate * (0.5 * (1.0 + bend)) * up).astype(BF16)
            h_ref[rows, :] = hidden
            target[...] = product(hidden, wd_ref[0]).astype(BF16)

    return kernel_call(
        body,
        [shape(half, width, BF16)] * 2
        + [shape(length, hidden_width, F32)] * 2
        + [shape(length, hidden_width, BF16)],
        (own, received, w_gate, w_up, w_down),
        {2: layer, 3: layer, 4: layer},
        flops=1_000_000_000,
    )


def feed_forward_back(own, received, weights, gate, up, layer):
    half, width = own.shape
    w_gate, w_up, w_down = weights
    hidden_width = w_gate.shape[2]
    length = 2 * half

    def body(
        own_ref, received_ref, wg_ref, wu_ref, wd_ref, g_ref, u_ref,
        kept_ref, sent_ref, gate_low_ref, up_low_ref,
    ):
        for part, source, target in ((1, received_ref, sent_ref), (0, own_ref, kept_ref)):
            rows = slice(part * half, (part + 1) * half)
            grad_hidden = product_right(source[...], wd_ref[0])
            gate_in = g_ref[rows, :]
            square = gate_in * gate_in
            bend = jnp.tanh(gelu_slope * gate_in * (1.0 + gelu_cubic * square))
            lift = 0.5 * (1.0 + bend)
            slope = lift + 0.5 * gate_in * (1.0 - bend * bend) * (
                gelu_slope * (1.0 + 3.0 * gelu_cubic * square)
            )
            gate_low = (grad_hidden * u_ref[rows, :] * slope).astype(BF16)
            up_low = (grad_hidden * (gate_in * lift)).astype(BF16)
            gate_low_ref[rows, :] = gate_low
            up_low_ref[rows, :] = up_low
            target[...] = (
                product_right(gate_low, wg_ref[0]) + product_right(up_low, wu_ref[0])
            ).astype(BF16)

    return kernel_call(
        body,
        [shape(half, width, BF16)] * 2 + [shape(length, hidden_width, BF16)] * 2,
        (own, received, w_gate, w_up, w_down, gate, up),
        {2: layer, 3: layer, 4: layer},
        flops=1_000_000_000,
    )


def attention_back(own, received, weights, tables, saved, layer, window):
    w_query, w_key, w_value, w_out, qk_gains = weights
    cosine, sine, down, across = tables
    query_raw, key_raw, queries, key_rows, values, row_lse = saved
    half, width = own.shape
    length = 2 * half
    head_width = w_key.shape[2]

    def body(
        own_ref, received_ref, wq_ref, wk_ref, wv_ref, wo_ref, gain_ref,
        cos_ref, sin_ref, down_ref, across_ref,
        qraw_ref, kraw_ref, q_ref, k_ref, v_ref, lse_ref,
        kept_ref, sent_ref, gq_ref, gk_ref, gv_ref, qgain_ref, kgain_ref,
    ):
        grad_keys = None
        grad_values = None
        query_gain = None
        for part, source in ((0, own_ref), (1, received_ref)):
            rows = slice(part * half, (part + 1) * half)
            grad_attended = product_right(source[...], wo_ref[0]).astype(BF16)
            queries_part = q_ref[rows, :]
            scores = product_right(queries_part, k_ref[...]) * score_scale
            allowed = allowed_rows(down_ref, across_ref, part * half, half, window)
            probability = jnp.where(allowed, jnp.exp(scores - lse_ref[rows, :]), 0.0)
            values_term = product_left(probability.astype(BF16), grad_attended)
            grad_prob = product_right(grad_attended, v_ref[...])
            inner_sum = jnp.sum(probability * grad_prob, axis=-1, keepdims=True)
            grad_scores = (probability * (grad_prob - inner_sum)).astype(BF16)
            keys_term = product_left(grad_scores, queries_part)
            grad_values = values_term if grad_values is None else grad_values + values_term
            grad_keys = keys_term if grad_keys is None else grad_keys + keys_term
            grad_queries = (product(grad_scores, k_ref[...]) * score_scale).astype(BF16)
            turned = rotate(grad_queries.astype(F32), cos_ref[rows, :], -sin_ref[rows, :])
            grad_raw, gain_term = norm_back(qraw_ref[rows, :], gain_ref[0, 0:1, :], turned)
            query_gain = gain_term if query_gain is None else query_gain + gain_term
            gq_ref[rows, :] = grad_raw.astype(BF16)
        qgain_ref[...] = query_gain
        grad_keys = (grad_keys * score_scale).astype(BF16)
        turned = rotate(grad_keys.astype(F32), cos_ref[...], -sin_ref[...])
        grad_raw, kgain_ref[...] = norm_back(kraw_ref[...], gain_ref[0, 1:2, :], turned)
        gk_ref[...] = grad_raw.astype(BF16)
        gv_ref[...] = grad_values.astype(BF16)
        for part, target in ((1, sent_ref), (0, kept_ref)):
            rows = slice(part * half, (part + 1) * half)
            target[...] = (
                product_right(gq_ref[rows, :], wq_ref[0])
                + product_right(gk_ref[rows, :], wk_ref[0])
                + product_right(gv_ref[rows, :], wv_ref[0])
            ).astype(BF16)

    return kernel_call(
        body,
        [shape(half, width, BF16)] * 2
        + [shape(length, head_width, BF16)] * 3
        + [shape(1, head_width, F32)] * 2,
        (
            own, received, w_query, w_key, w_value, w_out, qk_gains,
            cosine, sine, down, across, query_raw, key_raw, queries, key_rows, values, row_lse,
        ),
        {place: layer for place in (2, 3, 4, 5, 6)},
        flops=1_500_000_000,
    )


def slot_masks(bits):
    count = len(bits)
    return [
        sum(bit for place, bit in enumerate(bits) if slot >> (count - 1 - place) & 1)
        for slot in range(1 << count)
    ]


def gradient_blocks(factors, me, bits):
    pieces = 1 << len(bits)
    masks = slot_masks(bits)
    sizes = [(l[0].shape[1] // pieces, r[0].shape[1] // LANES) for l, r in factors]
    rows = sum(tall * wide for tall, wide in sizes)
    if any(tall % 16 for tall, wide in sizes):
        chunks = me[0] ^ jnp.array(masks, jnp.int32)
        parts = []
        for (left, right), (tall, wide) in zip(factors, sizes):
            grad = product_left(jnp.concatenate(left), jnp.concatenate(right)).astype(BF16)
            cut = grad.reshape(pieces, tall, wide, LANES).transpose(0, 2, 1, 3)
            parts.append(cut.reshape(pieces, tall * wide, LANES))
        blocks = jnp.take(jnp.concatenate(parts, axis=1), chunks, axis=0)
        return (blocks[: pieces // 2], blocks[pieces // 2 :])
    flat = []
    where = []
    for pair in factors:
        places = []
        for side in pair:
            places.append(list(range(len(flat), len(flat) + len(side))))
            flat.extend(side)
        where.append(places)

    def body(*refs):
        me_ref, inputs, (kept_ref, sent_ref, *scratch) = refs[0], refs[1 : 1 + len(flat)], refs[1 + len(flat) :]
        base = 0
        for (lefts, rights), (tall, wide), held in zip(where, sizes, scratch):
            def side(places):
                arrays = [inputs[place][...] for place in places]
                return arrays[0] if len(arrays) == 1 else jnp.concatenate(arrays, axis=0)

            held[...] = product_left(side(lefts), side(rights))
            for slot, mask in enumerate(masks):
                chunk = jnp.bitwise_xor(me_ref[0], mask)
                start = pl.multiple_of(chunk * tall, tall)
                target = kept_ref if slot < pieces // 2 else sent_ref
                block = held[pl.ds(start, tall), :].astype(BF16)
                for column in range(wide):
                    low = base + column * tall
                    target[slot % (pieces // 2), low : low + tall, :] = block[
                        :, column * LANES : (column + 1) * LANES
                    ]
            base += tall * wide

    out = jax.ShapeDtypeStruct((pieces // 2, rows, LANES), BF16)
    args = (me, *flat)
    specs = [pl.BlockSpec(memory_space=pltpu.SMEM)] + [
        pl.BlockSpec(a.shape, lambda i: (0, 0)) for a in flat
    ]
    return pl.pallas_call(
        body,
        grid=(1,),
        in_specs=specs,
        out_specs=[pl.BlockSpec(out.shape, lambda i: (0, 0, 0))] * 2,
        out_shape=[out, out],
        scratch_shapes=[
            pltpu.VMEM((tall * pieces, wide * LANES), F32) for tall, wide in sizes
        ],
        compiler_params=pltpu.CompilerParams(vmem_limit_bytes=40 << 20),
        cost_estimate=pl.CostEstimate(
            flops=1_000_000_000,
            transcendentals=0,
            bytes_accessed=sum(a.size * a.dtype.itemsize for a in args),
        ),
    )(*args)


def halved(blocks, bits):
    kept, sent = blocks
    for bit in bits[:-1]:
        arrived = swap(sent, "dp", bit)
        middle = kept.shape[0] // 2
        sent = (kept[middle:].astype(F32) + arrived[middle:].astype(F32)).astype(BF16)
        kept = kept[:middle].astype(F32) + arrived[:middle].astype(F32)
    return kept[0].astype(F32) + swap(sent, "dp", bits[-1])[0].astype(F32)


def over_tensor(rows):
    for bit in (1, 2):
        low = rows.astype(BF16)
        rows = low.astype(F32) + swap(low, "tensor", bit).astype(F32)
    return rows


def over_all(rows):
    bit = 1
    while bit < lax.axis_size("dp"):
        low = rows.astype(BF16)
        rows = low.astype(F32) + swap(low, "dp", bit).astype(F32)
        bit *= 2
    return over_tensor(rows)


def assembled(sources, layout, tall_of, columns_of):
    outs = [
        jax.ShapeDtypeStruct((2, tall, columns), F32)
        for tall, columns in zip(tall_of, columns_of)
    ]

    def cut(read, start, tall, columns):
        return [
            read(start + column * tall, tall) for column in range(columns // LANES)
        ]

    if any(tall % 8 for tall in tall_of):
        results = []
        for member, (tall, columns) in enumerate(zip(tall_of, columns_of)):
            both = [
                jnp.concatenate(
                    cut(lambda a, n: sources[source][a : a + n], start, tall, columns), axis=1
                )
                for source, start in layout[member]
            ]
            results.append(jnp.stack(both))
        return results

    def body(*refs):
        inputs, targets = refs[: len(sources)], refs[len(sources) :]
        for member, (tall, columns) in enumerate(zip(tall_of, columns_of)):
            for layer, (source, start) in enumerate(layout[member]):
                for column in range(columns // LANES):
                    low = start + column * tall
                    targets[member][layer, :, column * LANES : (column + 1) * LANES] = inputs[
                        source
                    ][low : low + tall, :]

    return pl.pallas_call(
        body,
        grid=(1,),
        in_specs=[pl.BlockSpec(a.shape, lambda i: (0, 0)) for a in sources],
        out_specs=[pl.BlockSpec(o.shape, lambda i: (0, 0, 0)) for o in outs],
        out_shape=outs,
        compiler_params=pltpu.CompilerParams(vmem_limit_bytes=40 << 20),
    )(*sources)


def local(
    hidden_in,
    cotangent,
    segments,
    positions,
    w_query,
    w_key,
    w_value,
    w_out,
    w_gate,
    w_up,
    w_down,
    norm_gains,
    qk_gains,
):
    head_width = w_key.shape[2]
    windows = (WINDOW, SEQ_LEN)
    pieces = lax.axis_size("dp")
    quarter = lax.axis_index("tensor")
    me = lax.axis_index("dp").astype(jnp.int32).reshape(1)
    bits = [1 << place for place in range(pieces.bit_length() - 1)]
    turned_bits = bits[1::-1] + bits[2:]
    seg_rows = relative_order(segments, quarter)
    pos_rows = relative_order(positions, quarter)
    places = relative_order(jnp.arange(SEQ_LEN, dtype=jnp.int32), quarter)
    down = jnp.stack([seg_rows, places], axis=1)
    across = jnp.stack([seg_rows, places], axis=0)
    attn_weights = (w_query, w_key, w_value, w_out, qk_gains)
    mlp_weights = (w_gate, w_up, w_down)
    tables = [angles(pos_rows, head_width, theta) + (down, across) for theta in thetas]

    stream = two_quarters(hidden_in)
    low = first_norm(stream, norm_gains, 0)
    saved = []
    for layer in range(2):
        received = swap(low, "tensor", 1)
        kept, sent, *kept_attn = attention(
            low, received, attn_weights, tables[layer], layer, windows[layer]
        )
        attn_in = (low, received)
        pair, other = summed_pair(kept, sent)
        attn_sum, middle, low = after_attention(pair, other, stream, norm_gains, layer)
        received = swap(low, "tensor", 1)
        kept, sent, *kept_mlp = feed_forward(low, received, mlp_weights, layer)
        mlp_in = (low, received)
        pair, other = summed_pair(kept, sent)
        saved.append([attn_in, kept_attn, attn_sum, middle, mlp_in, kept_mlp, stream])
        if layer == 0:
            mlp_sum, stream, low = between_layers(pair, other, middle, norm_gains, layer)

    grad_stream = two_quarters(cotangent)
    output, low, gain3 = turn_around(pair, other, middle, grad_stream, norm_gains, 1)
    sums = [None, None]
    gain_rows = [None, None]
    for layer in (1, 0):
        attn_in, kept_attn, attn_sum, middle, mlp_in, kept_mlp, stream = saved[layer]
        gate, up, hidden = kept_mlp
        query_raw, key_raw, queries, key_rows, values, attended, row_lse = kept_attn
        received = swap(low, "tensor", 1)
        kept, sent, gate_low, up_low = feed_forward_back(
            low, received, mlp_weights, gate, up, layer
        )
        mlp_out = (low, received)
        pair, other = summed_pair(kept, sent)
        mlp_order = bits if layer == 1 else turned_bits
        mlp_blocks = gradient_blocks(
            [(mlp_in, (gate_low,)), (mlp_in, (up_low,)), ((hidden,), mlp_out)], me, mlp_order
        )
        grad_middle, low, gain1, gain2 = back_to_attention(
            pair, other, middle, attn_sum, grad_stream, norm_gains, layer
        )
        received = swap(low, "tensor", 1)
        kept, sent, grad_q, grad_k, grad_v, gain_q, gain_k = attention_back(
            low,
            received,
            attn_weights,
            tables[layer],
            (query_raw, key_raw, queries, key_rows, values, row_lse),
            layer,
            windows[layer],
        )
        pair, other = summed_pair(kept, sent)
        attn_order = turned_bits if layer == 1 else bits
        attn_blocks = gradient_blocks(
            [
                (attn_in, (grad_q,)),
                ((attended,), (low, received)),
                (attn_in, (grad_k,)),
                (attn_in, (grad_v,)),
            ],
            me,
            attn_order,
        )
        sums[layer] = (halved(mlp_blocks, mlp_order), halved(attn_blocks, attn_order))
        gain_rows[layer] = [None, gain1, gain2, gain3, gain_q, gain_k]
        if layer == 1:
            grad_stream, low, gain_rows[1][0], gain3 = back_between(
                pair, other, stream, grad_middle, mlp_sum, norm_gains, layer
            )
        else:
            grad_input, gain_rows[0][0] = back_to_input(
                pair, other, stream, grad_middle, norm_gains, layer
            )

    width = norm_gains.shape[2]
    gain_terms = jnp.concatenate(
        [
            jnp.pad(row * 0.5 if place < 4 else row, ((0, 0), (0, width - row.shape[1])))
            for layer in range(2)
            for place, row in enumerate(gain_rows[layer])
        ]
    )
    gains = over_all(gain_terms).reshape(2, 6, width)

    def own_columns(array, columns):
        return lax.dynamic_slice_in_dim(array[:, :, :columns], me[0] * (columns // pieces), columns // pieces, 2)

    grad_norm_gains = own_columns(gains[:, :4], width)
    grad_qk_gains = own_columns(gains[:, 4:], head_width)

    tall = {
        "q": w_query.shape[1] // pieces,
        "o": w_out.shape[1] // pieces,
        "g": w_gate.shape[1] // pieces,
        "d": w_down.shape[1] // pieces,
    }
    heads_rows = tall["q"] * head_width // LANES
    out_rows = tall["o"] * w_out.shape[2] // LANES
    gate_rows = tall["g"] * w_gate.shape[2] // LANES
    shared = [over_tensor(sums[layer][1][heads_rows + out_rows :]) for layer in range(2)]
    sources = [sums[0][0], sums[1][0], sums[0][1], sums[1][1], shared[0], shared[1]]
    layout = [
        [(2, 0), (3, 0)],
        [(4, 0), (5, 0)],
        [(4, heads_rows), (5, heads_rows)],
        [(2, heads_rows), (3, heads_rows)],
        [(0, 0), (1, 0)],
        [(0, gate_rows), (1, gate_rows)],
        [(0, 2 * gate_rows), (1, 2 * gate_rows)],
    ]
    grads = assembled(
        sources,
        layout,
        [tall["q"], tall["q"], tall["q"], tall["o"], tall["g"], tall["g"], tall["d"]],
        [head_width] * 3 + [w_out.shape[2], w_gate.shape[2], w_up.shape[2], w_down.shape[2]],
    )
    return (output, grad_input, *grads, grad_norm_gains, grad_qk_gains)


def solution(mesh):
    return jax.shard_map(
        local,
        mesh=mesh,
        in_specs=(
            P(("dp", "tensor"), None),
            P(("dp", "tensor"), None),
            P("dp"),
            P("dp"),
            P(None, None, "tensor"),
            P(),
            P(),
            P(None, "tensor", None),
            P(None, None, "tensor"),
            P(None, None, "tensor"),
            P(None, "tensor", None),
            P(),
            P(),
        ),
        out_specs=(
            P(("dp", "tensor"), None),
            P(("dp", "tensor"), None),
            P(None, "dp", "tensor"),
            P(None, "dp", None),
            P(None, "dp", None),
            P(None, ("tensor", "dp"), None),
            P(None, "dp", "tensor"),
            P(None, "dp", "tensor"),
            P(None, ("tensor", "dp"), None),
            P(None, None, "dp"),
            P(None, None, "dp"),
        ),
        check_vma=False,
    )
```

```python
import jax
import jax.numpy as jnp
from jax import lax
from jax.experimental import pallas as pl
from jax.experimental.pallas import tpu as pltpu
from jax.sharding import PartitionSpec as P

WINDOW = 512
SEQ_LEN = 512
LANES = 128
VMEM_BYTES = 12 << 20
GAIN_ROWS = 16

epsilon = 1e-06
score_scale = 0.0625
masked_fill = -1e30
thetas = (10000.0, 1000000.0)
gelu_slope = 0.7978845608028654
gelu_cubic = 0.044715

F32 = jnp.float32
BF16 = jnp.bfloat16


def product(left, right):
    return jnp.dot(left, right, preferred_element_type=F32)


def product_left(left, right):
    return lax.dot_general(left, right, (((0,), (0,)), ((), ())), preferred_element_type=F32)


def product_right(left, right):
    return lax.dot_general(left, right, (((1,), (1,)), ((), ())), preferred_element_type=F32)


def angles(place, width, theta):
    half_width = width // 2
    frequency = theta ** (-(2.0 * jnp.arange(half_width, dtype=F32)) / width)
    phases = place.astype(F32)[:, None] * frequency[None, :]
    return (jnp.cos(phases), jnp.sin(phases))


def swap(array, axis, bit):
    size = lax.axis_size(axis)
    return lax.ppermute(array, axis, [(i, i ^ bit) for i in range(size)])


def relative_order(array, quarter):
    parts = array.reshape((4, -1) + array.shape[1:])
    return jnp.concatenate(
        [lax.dynamic_index_in_dim(parts, quarter ^ bit, 0, False) for bit in (0, 2, 1, 3)]
    )


def two_quarters(array):
    return jnp.concatenate([array, swap(array, "tensor", 2)])


def summed_pair(kept, sent):
    pair = (kept.astype(F32) + swap(sent, "tensor", 1).astype(F32)).astype(BF16)
    return (pair, swap(pair, "tensor", 2))


def kernel_call(body, outs, args, layers=None, scratch=()):
    layers = layers or {}

    def spec(place, arg):
        if place in layers:
            rest = arg.shape[1:]
            fixed = (layers[place],) + (0,) * len(rest)
            return pl.BlockSpec((1,) + rest, lambda i, fixed=fixed: fixed)
        if arg.shape == (1,):
            return pl.BlockSpec(memory_space=pltpu.SMEM)
        return pl.BlockSpec(arg.shape, lambda i, n=arg.ndim: (0,) * n)

    return pl.pallas_call(
        body,
        grid=(1,),
        in_specs=[spec(place, arg) for place, arg in enumerate(args)],
        out_specs=[pl.BlockSpec(o.shape, lambda i, n=len(o.shape): (0,) * n) for o in outs],
        out_shape=list(outs),
        scratch_shapes=list(scratch),
        compiler_params=pltpu.CompilerParams(vmem_limit_bytes=VMEM_BYTES),
        cost_estimate=pl.CostEstimate(flops=1, transcendentals=0, bytes_accessed=1),
    )(*args)


def shape(rows, columns, dtype):
    return jax.ShapeDtypeStruct((rows, columns), dtype)


def inverse_rms(vector):
    return lax.rsqrt(jnp.mean(vector * vector, axis=-1, keepdims=True) + epsilon)


def norm_forward(vector, gain_row):
    return vector * inverse_rms(vector) * gain_row


def norm_back(vector, gain_row, grad_out):
    scale = inverse_rms(vector)
    scaled = grad_out * gain_row
    inner = jnp.mean(scaled * vector, axis=-1, keepdims=True)
    grad = scale * scaled - vector * (scale * scale * scale * inner)
    grad_gain = jnp.sum(grad_out * (vector * scale), axis=0, keepdims=True)
    return (grad, grad_gain)


def rotate(vector, cosine, sine):
    half_width = vector.shape[-1] // 2
    first_half = vector[:, :half_width]
    second_half = vector[:, half_width:]
    return jnp.concatenate(
        [first_half * cosine - second_half * sine, second_half * cosine + first_half * sine],
        axis=-1,
    )


def total(pair_ref, other_ref):
    quarter = pair_ref.shape[0] // 2
    other = jnp.concatenate([other_ref[quarter:, :], other_ref[:quarter, :]], axis=0)
    return pair_ref[...].astype(F32) + other.astype(F32)


def first_norm(stream, gains, layer):
    def body(stream_ref, gains_ref, normed_ref):
        normed_ref[...] = norm_forward(
            stream_ref[...].astype(F32), gains_ref[0, 0:1, :]
        ).astype(BF16)

    return kernel_call(body, [shape(*stream.shape, BF16)], (stream, gains), {1: layer})[0]


def after_attention(pair, other, stream, gains, layer):
    def body(pair_ref, other_ref, stream_ref, gains_ref, sum_ref, middle_ref, normed_ref):
        attn_sum = total(pair_ref, other_ref)
        middle = stream_ref[...].astype(F32) + norm_forward(attn_sum, gains_ref[0, 1:2, :])
        sum_ref[...] = attn_sum
        middle_ref[...] = middle
        normed_ref[...] = norm_forward(middle, gains_ref[0, 2:3, :]).astype(BF16)

    size = pair.shape
    return kernel_call(
        body,
        [shape(*size, F32), shape(*size, F32), shape(*size, BF16)],
        (pair, other, stream, gains),
        {3: layer},
    )


def between_layers(pair, other, middle, gains, layer):
    def body(pair_ref, other_ref, middle_ref, gains_ref, next_ref, sum_ref, result_ref, low_ref):
        mlp_sum = total(pair_ref, other_ref)
        result = middle_ref[...] + norm_forward(mlp_sum, gains_ref[0, 3:4, :])
        sum_ref[...] = mlp_sum
        result_ref[...] = result
        low_ref[...] = norm_forward(result, next_ref[0, 0:1, :]).astype(BF16)

    size = pair.shape
    return kernel_call(
        body,
        [shape(*size, F32), shape(*size, F32), shape(*size, BF16)],
        (pair, other, middle, gains, gains),
        {3: layer, 4: layer + 1},
    )


def turn_around(pair, other, middle, cotangent, gains, layer):
    def body(pair_ref, other_ref, middle_ref, grad_ref, gains_ref, out_ref, low_ref, gain_ref):
        mlp_sum = total(pair_ref, other_ref)
        gain_row = gains_ref[0, 3:4, :]
        own = out_ref.shape[0]
        result = middle_ref[:own, :] + norm_forward(mlp_sum[:own, :], gain_row)
        out_ref[...] = result.astype(BF16)
        grad, grad_gain = norm_back(mlp_sum, gain_row, grad_ref[...].astype(F32))
        low_ref[...] = grad.astype(BF16)
        gain_ref[...] = grad_gain

    rows, columns = pair.shape
    return kernel_call(
        body,
        [shape(rows // 2, columns, BF16), shape(rows, columns, BF16), shape(1, columns, F32)],
        (pair, other, middle, cotangent, gains),
        {4: layer},
    )


def back_to_attention(pair, other, middle, attn_sum, grad_stream, gains, layer):
    def body(
        pair_ref, other_ref, middle_ref, attn_ref, grad_ref, gains_ref,
        grad_middle_ref, low_ref, gain1_ref, gain2_ref,
    ):
        grad_normed = total(pair_ref, other_ref)
        step, gain2_ref[...] = norm_back(middle_ref[...], gains_ref[0, 2:3, :], grad_normed)
        grad_middle = grad_ref[...].astype(F32) + step
        grad_middle_ref[...] = grad_middle
        grad_attn, gain1_ref[...] = norm_back(attn_ref[...], gains_ref[0, 1:2, :], grad_middle)
        low_ref[...] = grad_attn.astype(BF16)

    rows, columns = pair.shape
    return kernel_call(
        body,
        [shape(rows, columns, F32), shape(rows, columns, BF16)] + [shape(1, columns, F32)] * 2,
        (pair, other, middle, attn_sum, grad_stream, gains),
        {5: layer},
    )


def back_between(pair, other, stream, grad_middle, mlp_sum, gains, layer):
    def body(
        pair_ref, other_ref, stream_ref, grad_ref, mlp_ref, gains_ref, below_ref,
        grad_stream_ref, low_ref, gain0_ref, gain3_ref,
    ):
        grad_normed = total(pair_ref, other_ref)
        step, gain0_ref[...] = norm_back(stream_ref[...], gains_ref[0, 0:1, :], grad_normed)
        grad_stream = grad_ref[...] + step
        grad_stream_ref[...] = grad_stream
        grad_mlp, gain3_ref[...] = norm_back(mlp_ref[...], below_ref[0, 3:4, :], grad_stream)
        low_ref[...] = grad_mlp.astype(BF16)

    rows, columns = pair.shape
    return kernel_call(
        body,
        [shape(rows, columns, F32), shape(rows, columns, BF16)] + [shape(1, columns, F32)] * 2,
        (pair, other, stream, grad_middle, mlp_sum, gains, gains),
        {5: layer, 6: layer - 1},
    )


def back_to_input(pair, other, stream, grad_middle, gains, layer):
    def body(pair_ref, other_ref, stream_ref, grad_ref, gains_ref, out_ref):
        own = out_ref.shape[0]
        grad_normed = pair_ref[:own, :].astype(F32) + other_ref[own:, :].astype(F32)
        step, unused = norm_back(
            stream_ref[:own, :].astype(F32), gains_ref[0, 0:1, :], grad_normed
        )
        out_ref[...] = (grad_ref[:own, :] + step).astype(BF16)

    rows, columns = pair.shape
    return kernel_call(
        body,
        [shape(rows // 2, columns, BF16)],
        (pair, other, stream, grad_middle, gains),
        {4: layer},
    )[0]


def allowed_rows(down_ref, across_ref, start, count, window):
    seg_down = down_ref[start : start + count, 0:1]
    place_down = down_ref[start : start + count, 1:2]
    seg_across = across_ref[0:1, :]
    place_across = across_ref[1:2, :]
    allowed = (seg_down == seg_across) & (place_across <= place_down)
    if window < SEQ_LEN:
        allowed = allowed & (place_down - place_across < window)
    return allowed


def attention(own, received, weights, tables, layer, window):
    w_query, w_key, w_value, w_out, qk_gains = weights
    cosine, sine, down, across = tables
    half = own.shape[0]
    length = 2 * half
    head_width = w_key.shape[2]

    def body(
        own_ref, received_ref, wq_ref, wk_ref, wv_ref, wo_ref, gain_ref,
        cos_ref, sin_ref, down_ref, across_ref,
        kept_ref, sent_ref, qraw_ref, kraw_ref, q_ref, k_ref, v_ref, attended_ref, lse_ref,
    ):
        for part, source in ((0, own_ref), (1, received_ref)):
            rows = slice(part * half, (part + 1) * half)
            normed = source[...]
            cos_rows, sin_rows = cos_ref[rows, :], sin_ref[rows, :]
            key_raw = product(normed, wk_ref[0])
            kraw_ref[rows, :] = key_raw
            k_ref[rows, :] = rotate(
                norm_forward(key_raw, gain_ref[0, 1:2, :]), cos_rows, sin_rows
            ).astype(BF16)
            v_ref[rows, :] = product(normed, wv_ref[0]).astype(BF16)
            query_raw = product(normed, wq_ref[0])
            qraw_ref[rows, :] = query_raw
            q_ref[rows, :] = rotate(
                norm_forward(query_raw, gain_ref[0, 0:1, :]), cos_rows, sin_rows
            ).astype(BF16)
        for part, target in ((1, sent_ref), (0, kept_ref)):
            rows = slice(part * half, (part + 1) * half)
            scores = product_right(q_ref[rows, :], k_ref[...]) * score_scale
            allowed = allowed_rows(down_ref, across_ref, part * half, half, window)
            masked = jnp.where(allowed, scores, masked_fill)
            row_max = jnp.max(masked, axis=-1, keepdims=True)
            expo = jnp.where(allowed, jnp.exp(masked - row_max), 0.0)
            row_sum = jnp.sum(expo, axis=-1, keepdims=True)
            probability = (expo * (1.0 / row_sum)).astype(BF16)
            lse_ref[rows, :] = row_max + jnp.log(row_sum)
            attended = product(probability, v_ref[...]).astype(BF16)
            attended_ref[rows, :] = attended
            target[...] = product(attended, wo_ref[0]).astype(BF16)

    width = own.shape[1]
    return kernel_call(
        body,
        [shape(half, width, BF16)] * 2
        + [shape(length, head_width, F32)] * 2
        + [shape(length, head_width, BF16)] * 4
        + [shape(length, 1, F32)],
        (own, received, w_query, w_key, w_value, w_out, qk_gains, cosine, sine, down, across),
        {place: layer for place in (2, 3, 4, 5, 6)},
    )


def feed_forward(own, received, weights, layer):
    half, width = own.shape
    w_gate, w_up, w_down = weights
    hidden_width = w_gate.shape[2]
    length = 2 * half

    def body(own_ref, received_ref, wg_ref, wu_ref, wd_ref, kept_ref, sent_ref, g_ref, u_ref, h_ref):
        for part, source, target in ((1, received_ref, sent_ref), (0, own_ref, kept_ref)):
            rows = slice(part * half, (part + 1) * half)
            normed = source[...]
            gate = product(normed, wg_ref[0])
            up = product(normed, wu_ref[0])
            g_ref[rows, :] = gate
            u_ref[rows, :] = up
            bend = jnp.tanh(gelu_slope * (gate + gelu_cubic * (gate * gate * gate)))
            hidden = (gate * (0.5 * (1.0 + bend)) * up).astype(BF16)
            h_ref[rows, :] = hidden
            target[...] = product(hidden, wd_ref[0]).astype(BF16)

    return kernel_call(
        body,
        [shape(half, width, BF16)] * 2
        + [shape(length, hidden_width, F32)] * 2
        + [shape(length, hidden_width, BF16)],
        (own, received, w_gate, w_up, w_down),
        {2: layer, 3: layer, 4: layer},
    )


def feed_forward_back(own, received, weights, gate, up, layer):
    half, width = own.shape
    w_gate, w_up, w_down = weights
    hidden_width = w_gate.shape[2]
    length = 2 * half

    def body(
        own_ref, received_ref, wg_ref, wu_ref, wd_ref, g_ref, u_ref,
        kept_ref, sent_ref, gate_low_ref, up_low_ref,
    ):
        for part, source, target in ((1, received_ref, sent_ref), (0, own_ref, kept_ref)):
            rows = slice(part * half, (part + 1) * half)
            grad_hidden = product_right(source[...], wd_ref[0])
            gate_in = g_ref[rows, :]
            square = gate_in * gate_in
            bend = jnp.tanh(gelu_slope * gate_in * (1.0 + gelu_cubic * square))
            lift = 0.5 * (1.0 + bend)
            slope = lift + 0.5 * gate_in * (1.0 - bend * bend) * (
                gelu_slope * (1.0 + 3.0 * gelu_cubic * square)
            )
            gate_low = (grad_hidden * u_ref[rows, :] * slope).astype(BF16)
            up_low = (grad_hidden * (gate_in * lift)).astype(BF16)
            gate_low_ref[rows, :] = gate_low
            up_low_ref[rows, :] = up_low
            target[...] = (
                product_right(gate_low, wg_ref[0]) + product_right(up_low, wu_ref[0])
            ).astype(BF16)

    return kernel_call(
        body,
        [shape(half, width, BF16)] * 2 + [shape(length, hidden_width, BF16)] * 2,
        (own, received, w_gate, w_up, w_down, gate, up),
        {2: layer, 3: layer, 4: layer},
    )


def attention_back(own, received, weights, tables, saved, side, layer, window, first=()):
    w_query, w_key, w_value, w_out, qk_gains = weights
    cosine, sine, down, across = tables
    query_raw, key_raw, queries, key_rows, values, row_lse = saved
    half, width = own.shape
    length = 2 * half
    head_width = w_key.shape[2]

    def body(
        own_ref, received_ref, wq_ref, wk_ref, wv_ref, wo_ref, gain_ref,
        cos_ref, sin_ref, down_ref, across_ref,
        qraw_ref, kraw_ref, q_ref, k_ref, v_ref, lse_ref, side_ref,
        *rest,
    ):
        firsts, rest = rest[: len(first)], rest[len(first) :]
        kept_ref, sent_ref, gq_ref, mine_ref, theirs_ref, qgain_ref, kgain_ref = rest[:7]
        *gain0_refs, gk_ref, gv_ref = rest[7:]
        grad_keys = None
        grad_values = None
        query_gain = None
        for part, source in ((0, own_ref), (1, received_ref)):
            rows = slice(part * half, (part + 1) * half)
            grad_attended = product_right(source[...], wo_ref[0]).astype(BF16)
            queries_part = q_ref[rows, :]
            scores = product_right(queries_part, k_ref[...]) * score_scale
            allowed = allowed_rows(down_ref, across_ref, part * half, half, window)
            probability = jnp.where(allowed, jnp.exp(scores - lse_ref[rows, :]), 0.0)
            values_term = product_left(probability.astype(BF16), grad_attended)
            grad_prob = product_right(grad_attended, v_ref[...])
            inner_sum = jnp.sum(probability * grad_prob, axis=-1, keepdims=True)
            grad_scores = (probability * (grad_prob - inner_sum)).astype(BF16)
            keys_term = product_left(grad_scores, queries_part)
            grad_values = values_term if grad_values is None else grad_values + values_term
            grad_keys = keys_term if grad_keys is None else grad_keys + keys_term
            grad_queries = (product(grad_scores, k_ref[...]) * score_scale).astype(BF16)
            turned = rotate(grad_queries.astype(F32), cos_ref[rows, :], -sin_ref[rows, :])
            grad_raw, gain_term = norm_back(qraw_ref[rows, :], gain_ref[0, 0:1, :], turned)
            query_gain = gain_term if query_gain is None else query_gain + gain_term
            gq_ref[rows, :] = grad_raw.astype(BF16)
        qgain_ref[...] = query_gain
        grad_keys = (grad_keys * score_scale).astype(BF16)
        turned = rotate(grad_keys.astype(F32), cos_ref[...], -sin_ref[...])
        grad_raw, kgain_ref[...] = norm_back(kraw_ref[...], gain_ref[0, 1:2, :], turned)
        gk_ref[...] = grad_raw.astype(BF16)
        gv_ref[...] = grad_values.astype(BF16)

        @pl.when(side_ref[0] == 0)
        def keys_here():
            mine_ref[...] = gk_ref[...]
            theirs_ref[...] = gv_ref[...]

        @pl.when(side_ref[0] != 0)
        def values_here():
            mine_ref[...] = gv_ref[...]
            theirs_ref[...] = gk_ref[...]

        for part, target in ((1, sent_ref), (0, kept_ref)):
            rows = slice(part * half, (part + 1) * half)
            target[...] = (
                product_right(gq_ref[rows, :], wq_ref[0])
                + product_right(gk_ref[rows, :], wk_ref[0])
                + product_right(gv_ref[rows, :], wv_ref[0])
            ).astype(BF16)
        if first:
            low_ref, other_ref, norm_ref = firsts
            gain0_refs[0][...] = (
                jnp.sum(
                    kept_ref[...].astype(F32) * low_ref[...].astype(F32)
                    + sent_ref[...].astype(F32) * other_ref[...].astype(F32),
                    axis=0,
                    keepdims=True,
                )
                / norm_ref[0, 0:1, :]
            )

    fixed = {place: layer for place in (2, 3, 4, 5, 6)}
    if first:
        fixed[20] = layer
    return kernel_call(
        body,
        [shape(half, width, BF16)] * 2
        + [shape(length, head_width, BF16)] * 3
        + [shape(1, head_width, F32)] * 2
        + [shape(1, width, F32)] * (1 if first else 0),
        (
            own, received, w_query, w_key, w_value, w_out, qk_gains,
            cosine, sine, down, across, query_raw, key_raw, queries, key_rows, values, row_lse, side,
            *first,
        ),
        fixed,
        scratch=[pltpu.VMEM((length, head_width), BF16)] * 2,
    )


def slot_masks(bits):
    count = len(bits)
    return [
        sum(bit for place, bit in enumerate(bits) if slot >> (count - 1 - place) & 1)
        for slot in range(1 << count)
    ]


def gradient_blocks(factors, me, bits, gains=()):
    pieces = 1 << len(bits)
    masks = slot_masks(bits)
    sizes = [(l[0].shape[1] // pieces, r[0].shape[1] // LANES) for l, r in factors]
    rows = sum(tall * wide for tall, wide in sizes)
    if any(tall % 16 for tall, wide in sizes):
        chunks = me[0] ^ jnp.array(masks, jnp.int32)
        parts = []
        for (left, right), (tall, wide) in zip(factors, sizes):
            grad = product_left(jnp.concatenate(left), jnp.concatenate(right)).astype(BF16)
            cut = grad.reshape(pieces, tall, wide, LANES).transpose(0, 2, 1, 3)
            parts.append(cut.reshape(pieces, tall * wide, LANES))
        if gains:
            rows = [
                jnp.pad(row.reshape(pieces, 1, -1), ((0, 0), (0, 0), (0, LANES - row.shape[1] // pieces)))
                for row in gains
            ]
            block = jnp.concatenate(rows, axis=1)
            parts.append(
                jnp.pad(block, ((0, 0), (0, GAIN_ROWS - len(rows)), (0, 0))).astype(BF16)
            )
        blocks = jnp.take(jnp.concatenate(parts, axis=1), chunks, axis=0)
        return (blocks[: pieces // 2], blocks[pieces // 2 :])
    flat = []
    where = []
    for pair in factors:
        places = []
        for side in pair:
            places.append(list(range(len(flat), len(flat) + len(side))))
            flat.extend(side)
        where.append(places)

    def body(*refs):
        me_ref, inputs = refs[0], refs[1 : 1 + len(flat)]
        gain_refs = refs[1 + len(flat) : 1 + len(flat) + len(gains)]
        kept_ref, sent_ref, *scratch = refs[1 + len(flat) + len(gains) :]
        base = 0
        for (lefts, rights), (tall, wide), held in zip(where, sizes, scratch):
            def side(places):
                arrays = [inputs[place][...] for place in places]
                return arrays[0] if len(arrays) == 1 else jnp.concatenate(arrays, axis=0)

            held[...] = product_left(side(lefts), side(rights))
            for slot, mask in enumerate(masks):
                chunk = jnp.bitwise_xor(me_ref[0], mask)
                start = pl.multiple_of(chunk * tall, tall)
                target = kept_ref if slot < pieces // 2 else sent_ref
                block = held[pl.ds(start, tall), :].astype(BF16)
                for column in range(wide):
                    low = base + column * tall
                    target[slot % (pieces // 2), low : low + tall, :] = block[
                        :, column * LANES : (column + 1) * LANES
                    ]
            base += tall * wide
        if gains:
            table = scratch[-1]
            table[...] = jnp.zeros_like(table)
            for place, ref in enumerate(gain_refs):
                count = ref.shape[1] // pieces
                for chunk in range(pieces):
                    line = chunk * GAIN_ROWS + place
                    table[line : line + 1, :count] = ref[:, chunk * count : (chunk + 1) * count]
            for slot, mask in enumerate(masks):
                chunk = jnp.bitwise_xor(me_ref[0], mask)
                start = pl.multiple_of(chunk * GAIN_ROWS, GAIN_ROWS)
                target = kept_ref if slot < pieces // 2 else sent_ref
                target[slot % (pieces // 2), base : base + GAIN_ROWS, :] = table[
                    pl.ds(start, GAIN_ROWS), :
                ].astype(BF16)

    rows += GAIN_ROWS if gains else 0
    out = jax.ShapeDtypeStruct((pieces // 2, rows, LANES), BF16)
    args = (me, *flat, *gains)
    specs = [pl.BlockSpec(memory_space=pltpu.SMEM)] + [
        pl.BlockSpec(a.shape, lambda i: (0, 0)) for a in args[1:]
    ]
    return pl.pallas_call(
        body,
        grid=(1,),
        in_specs=specs,
        out_specs=[pl.BlockSpec(out.shape, lambda i: (0, 0, 0))] * 2,
        out_shape=[out, out],
        scratch_shapes=[
            pltpu.VMEM((tall * pieces, wide * LANES), F32) for tall, wide in sizes
        ]
        + [pltpu.VMEM((pieces * GAIN_ROWS, LANES), F32)] * (1 if gains else 0),
        compiler_params=pltpu.CompilerParams(vmem_limit_bytes=VMEM_BYTES),
        cost_estimate=pl.CostEstimate(flops=1, transcendentals=0, bytes_accessed=1),
    )(*args)


def after(gate, *values):
    return lax.optimization_barrier((gate,) + values)[1:]


class Halving:
    def __init__(self, terms, me, bits, gains=()):
        self.kept, sent = gradient_blocks(terms, me, bits, gains)
        self.bits = bits
        self.arrived = swap(sent, "dp", bits[0])

    def step(self, gate=None):
        if not self.bits:
            return
        kept, arrived = self.kept, self.arrived
        if gate is not None:
            kept, arrived = after(gate, kept, arrived)
        self.bits = self.bits[1:]
        if self.bits:
            middle = kept.shape[0] // 2
            sent = (kept[middle:].astype(F32) + arrived[middle:].astype(F32)).astype(BF16)
            self.arrived = swap(sent, "dp", self.bits[0])
            self.kept = kept[:middle].astype(F32) + arrived[:middle].astype(F32)
        else:
            self.kept = kept[0].astype(F32) + arrived[0].astype(F32)

    def finish(self):
        while self.bits:
            self.step()
        return self.kept


def assembled(sources, layout, sizes, exchanged, starts, shared_size, gains_at, gain_widths):
    sizes = sizes + [shared_size] * 2
    here, there, side = exchanged
    outs = [jax.ShapeDtypeStruct((2, tall, columns), F32) for tall, columns in sizes]
    outs += [
        jax.ShapeDtypeStruct((2, 4, gain_widths[0]), F32),
        jax.ShapeDtypeStruct((2, 2, gain_widths[1]), F32),
    ]

    if any(tall % 16 for tall, columns in sizes):

        def joined(array, start, tall, columns):
            return jnp.concatenate(
                [
                    array[start + place * tall : start + (place + 1) * tall]
                    for place in range(columns // LANES)
                ],
                axis=1,
            ).astype(F32)

        results = [
            jnp.stack([joined(sources[source], start, *size) for source, start in both])
            for both, size in zip(layout, sizes)
        ]
        for first, second in ((here, there), (there, here)):
            picked = jnp.where(side == 0, first, second)
            results.append(jnp.stack([joined(picked, start, *shared_size) for start in starts]))
        gains = here[gains_at : gains_at + GAIN_ROWS].astype(F32)
        gains = (gains + there[gains_at : gains_at + GAIN_ROWS].astype(F32))[:12]
        gains = gains.reshape(2, 6, LANES)
        return results + [gains[:, :4, : gain_widths[0]], gains[:, 4:, : gain_widths[1]]]

    def body(*refs):
        inputs = refs[: len(sources)]
        here_ref, there_ref, side_ref = refs[len(sources) : len(sources) + 3]
        *targets, norm_ref, qk_ref = refs[len(sources) + 3 :]

        def put(target, layer, source, start, tall, columns):
            for column in range(columns // LANES):
                low = start + column * tall
                target[layer, :, column * LANES : (column + 1) * LANES] = source[
                    low : low + tall, :
                ].astype(F32)

        for member, both in enumerate(layout):
            for layer, (source, start) in enumerate(both):
                put(targets[member], layer, inputs[source], start, *sizes[member])
        key_ref, value_ref = targets[-2:]

        @pl.when(side_ref[0] == 0)
        def keys_here():
            for layer, start in enumerate(starts):
                put(key_ref, layer, here_ref, start, *shared_size)
                put(value_ref, layer, there_ref, start, *shared_size)

        @pl.when(side_ref[0] != 0)
        def values_here():
            for layer, start in enumerate(starts):
                put(key_ref, layer, there_ref, start, *shared_size)
                put(value_ref, layer, here_ref, start, *shared_size)

        gains = here_ref[gains_at : gains_at + GAIN_ROWS, :].astype(F32)
        gains = gains + there_ref[gains_at : gains_at + GAIN_ROWS, :].astype(F32)
        for layer in range(2):
            norm_ref[layer] = gains[6 * layer : 6 * layer + 4, : gain_widths[0]]
            qk_ref[layer] = gains[6 * layer + 4 : 6 * layer + 6, : gain_widths[1]]

    return kernel_call(body, outs, (*sources, here, there, side))


def local(
    hidden_in,
    cotangent,
    segments,
    positions,
    w_query,
    w_key,
    w_value,
    w_out,
    w_gate,
    w_up,
    w_down,
    norm_gains,
    qk_gains,
):
    head_width = w_key.shape[2]
    windows = (WINDOW, SEQ_LEN)
    pieces = lax.axis_size("dp")
    quarter = lax.axis_index("tensor")
    me = lax.axis_index("dp").astype(jnp.int32).reshape(1)
    side = jnp.bitwise_and(quarter, 1).astype(jnp.int32).reshape(1)
    hidden_in, segments, positions, quarter, me, side = lax.optimization_barrier(
        (hidden_in, segments, positions, quarter, me, side)
    )
    bits = [1 << place for place in range(pieces.bit_length() - 1)]
    turned_bits = bits[1::-1] + bits[2:]
    seg_rows = relative_order(segments, quarter)
    pos_rows = relative_order(positions, quarter)
    places = relative_order(jnp.arange(SEQ_LEN, dtype=jnp.int32), quarter)
    down = jnp.stack([seg_rows, places], axis=1)
    across = jnp.stack([seg_rows, places], axis=0)
    attn_weights = (w_query, w_key, w_value, w_out, qk_gains)
    mlp_weights = (w_gate, w_up, w_down)
    tables = [angles(pos_rows, head_width, theta) + (down, across) for theta in thetas]

    stream = two_quarters(hidden_in)
    low = first_norm(stream, norm_gains, 0)
    saved = []
    for layer in range(2):
        received = swap(low, "tensor", 1)
        kept, sent, *kept_attn = attention(
            low, received, attn_weights, tables[layer], layer, windows[layer]
        )
        attn_in = (low, received)
        pair, other = summed_pair(kept, sent)
        attn_sum, middle, low = after_attention(pair, other, stream, norm_gains, layer)
        received = swap(low, "tensor", 1)
        kept, sent, *kept_mlp = feed_forward(low, received, mlp_weights, layer)
        mlp_in = (low, received)
        pair, other = summed_pair(kept, sent)
        saved.append([attn_in, kept_attn, attn_sum, middle, mlp_in, kept_mlp, stream])
        if layer == 0:
            mlp_sum, stream, low = between_layers(pair, other, middle, norm_gains, layer)

    grad_stream = two_quarters(cotangent)
    output, low, gain3 = turn_around(pair, other, middle, grad_stream, norm_gains, 1)
    sums = {}
    gain_rows = [None, None]
    for layer in (1, 0):
        attn_in, kept_attn, attn_sum, middle, mlp_in, kept_mlp, stream = saved[layer]
        gate, up, hidden = kept_mlp
        query_raw, key_raw, queries, key_rows, values, attended, row_lse = kept_attn
        received = swap(low, "tensor", 1)
        kept, sent, gate_low, up_low = feed_forward_back(
            low, received, mlp_weights, gate, up, layer
        )
        mlp_out = (low, received)
        pair, other = summed_pair(kept, sent)
        gate_low, up_low = after(pair, gate_low, up_low)
        gate_term, up_term = (mlp_in, (gate_low,)), (mlp_in, (up_low,))
        down_term = ((hidden,), mlp_out)
        if layer == 1:
            sums["mlp1"] = Halving([gate_term, up_term, down_term], me, bits)
            (other,) = after(sums["mlp1"].kept, other)
        else:
            sums["mlp0"] = Halving([gate_term, up_term, down_term], me, bits)
            made = sums["mlp0"].kept
            sums["mlp1"].step(made)
            sums["attn1"].step(made)
            (other,) = after([s.kept for s in sums.values()], other)
        grad_middle, low, gain1, gain2 = back_to_attention(
            pair, other, middle, attn_sum, grad_stream, norm_gains, layer
        )
        received = swap(low, "tensor", 1)
        kept, sent, grad_q, mine, theirs, gain_q, gain_k, *gain0 = attention_back(
            low,
            received,
            attn_weights,
            tables[layer],
            (query_raw, key_raw, queries, key_rows, values, row_lse),
            side,
            layer,
            windows[layer],
            () if layer else (*attn_in, norm_gains),
        )
        pair, other = summed_pair(kept, sent)
        theirs = swap(theirs, "tensor", 1)
        if layer == 1:
            grad_q, mine, theirs = after(pair, grad_q, mine, theirs)
        shared_term = (attn_in + attn_in[::-1], (mine, theirs))
        query_term, out_term = (attn_in, (grad_q,)), ((attended,), (low, received))
        gain_rows[layer] = [None, gain1 * 0.5, gain2 * 0.5, gain3 * 0.5, gain_q, gain_k]
        if layer == 1:
            sums["attn1"] = Halving([query_term, out_term, shared_term], me, bits)
            sums["mlp1"].step(sums["attn1"].kept)
            (other,) = after([s.kept for s in sums.values()], other)
            grad_stream, low, gain0, gain3 = back_between(
                pair, other, stream, grad_middle, mlp_sum, norm_gains, layer
            )
            gain_rows[1][0] = gain0 * 0.5
        else:
            gain_rows[0][0] = gain0[0]
            sums["attn0"] = Halving(
                [query_term, out_term, shared_term],
                me,
                turned_bits,
                gain_rows[0] + gain_rows[1],
            )
            for name in ("mlp1", "attn1", "mlp0"):
                sums[name].step(sums["attn0"].kept)
            grad_input = back_to_input(pair, other, stream, grad_middle, norm_gains, layer)

    sums["attn0"].step(sums["mlp0"].kept)
    sums["attn0"].step()
    sums["mlp0"].step(sums["attn0"].kept)
    sums["attn0"].finish()
    tall = {
        "q": w_query.shape[1] // pieces,
        "o": w_out.shape[1] // pieces,
        "g": w_gate.shape[1] // pieces,
        "d": w_down.shape[1] // pieces,
    }
    heads_rows = tall["q"] * head_width // LANES
    gate_rows = tall["g"] * w_gate.shape[2] // LANES
    both_rows = heads_rows + tall["o"] * w_out.shape[2] // LANES
    done = {name: halving.finish() for name, halving in sums.items()}
    low = jnp.concatenate([done["attn0"][both_rows:], done["attn1"][both_rows:]]).astype(BF16)
    here = (low.astype(F32) + swap(low, "tensor", 2).astype(F32)).astype(BF16)
    there = swap(here, "tensor", 1)
    first_rows = done["attn0"].shape[0] - both_rows
    *grads, grad_norm_gains, grad_qk_gains = assembled(
        [done[name] for name in ("attn0", "attn1", "mlp0", "mlp1")],
        [
            [(0, 0), (1, 0)],
            [(0, heads_rows), (1, heads_rows)],
            [(2, 0), (3, 0)],
            [(2, gate_rows), (3, gate_rows)],
            [(2, 2 * gate_rows), (3, 2 * gate_rows)],
        ],
        [(tall["q"], head_width), (tall["o"], w_out.shape[2])]
        + [(tall["g"], w_gate.shape[2])] * 2
        + [(tall["d"], w_down.shape[2])],
        (here, there, side),
        [0, first_rows],
        (tall["q"], head_width),
        first_rows - GAIN_ROWS,
        (norm_gains.shape[2] // pieces, head_width // pieces),
    )
    grad_query, grad_out, grad_gate, grad_up, grad_down, grad_key, grad_value = grads
    return (
        output,
        grad_input,
        grad_query,
        grad_key,
        grad_value,
        grad_out,
        grad_gate,
        grad_up,
        grad_down,
        grad_norm_gains,
        grad_qk_gains,
    )


def solution(mesh):
    return jax.shard_map(
        local,
        mesh=mesh,
        in_specs=(
            P(("dp", "tensor"), None),
            P(("dp", "tensor"), None),
            P("dp"),
            P("dp"),
            P(None, None, "tensor"),
            P(),
            P(),
            P(None, "tensor", None),
            P(None, None, "tensor"),
            P(None, None, "tensor"),
            P(None, "tensor", None),
            P(),
            P(),
        ),
        out_specs=(
            P(("dp", "tensor"), None),
            P(("dp", "tensor"), None),
            P(None, "dp", "tensor"),
            P(None, "dp", None),
            P(None, "dp", None),
            P(None, ("tensor", "dp"), None),
            P(None, "dp", "tensor"),
            P(None, "dp", "tensor"),
            P(None, ("tensor", "dp"), None),
            P(None, None, "dp"),
            P(None, None, "dp"),
        ),
        check_vma=False,
    )
```

```python
import jax
import jax.numpy as jnp
from jax import lax
from jax.experimental import pallas as pl
from jax.experimental.pallas import tpu as pltpu
from jax.sharding import PartitionSpec as P

WINDOW = 512
SEQ_LEN = 512
LANES = 128
VMEM_BYTES = 12 << 20
FORWARD_COST = (1_000_000_000, 4_000_000)
GAIN_ROWS = 16

epsilon = 1e-06
score_scale = 0.0625
masked_fill = -1e30
thetas = (10000.0, 1000000.0)
gelu_slope = 0.7978845608028654
gelu_cubic = 0.044715

F32 = jnp.float32
BF16 = jnp.bfloat16


def product(left, right):
    return jnp.dot(left, right, preferred_element_type=F32)


def product_left(left, right):
    return lax.dot_general(left, right, (((0,), (0,)), ((), ())), preferred_element_type=F32)


def product_right(left, right):
    return lax.dot_general(left, right, (((1,), (1,)), ((), ())), preferred_element_type=F32)


def swap(array, axis, bit):
    size = lax.axis_size(axis)
    return lax.ppermute(array, axis, [(i, i ^ bit) for i in range(size)])


def summed_pair(kept, sent):
    pair = (kept.astype(F32) + swap(sent, "tensor", 1).astype(F32)).astype(BF16)
    return (pair, swap(pair, "tensor", 2))


def kernel_call(body, outs, args, layers=None, scratch=(), cost=(1, 1)):
    layers = layers or {}

    def spec(place, arg):
        if place in layers:
            rest = arg.shape[1:]
            fixed = (layers[place],) + (0,) * len(rest)
            return pl.BlockSpec((1,) + rest, lambda i, fixed=fixed: fixed)
        if arg.shape == (1,):
            return pl.BlockSpec(memory_space=pltpu.SMEM)
        return pl.BlockSpec(arg.shape, lambda i, n=arg.ndim: (0,) * n)

    return pl.pallas_call(
        body,
        grid=(1,),
        in_specs=[spec(place, arg) for place, arg in enumerate(args)],
        out_specs=[pl.BlockSpec(o.shape, lambda i, n=len(o.shape): (0,) * n) for o in outs],
        out_shape=list(outs),
        scratch_shapes=list(scratch),
        compiler_params=pltpu.CompilerParams(vmem_limit_bytes=VMEM_BYTES),
        cost_estimate=pl.CostEstimate(
            flops=cost[0], transcendentals=0, bytes_accessed=cost[1]
        ),
    )(*args)


def shape(rows, columns, dtype):
    return jax.ShapeDtypeStruct((rows, columns), dtype)


def inverse_rms(vector):
    return lax.rsqrt(jnp.mean(vector * vector, axis=-1, keepdims=True) + epsilon)


def norm_forward(vector, gain_row):
    return vector * inverse_rms(vector) * gain_row


def norm_back(vector, gain_row, grad_out):
    scale = inverse_rms(vector)
    scaled = grad_out * gain_row
    inner = jnp.mean(scaled * vector, axis=-1, keepdims=True)
    grad = scale * scaled - vector * (scale * scale * scale * inner)
    grad_gain = jnp.sum(grad_out * (vector * scale), axis=0, keepdims=True)
    return (grad, grad_gain)


def rotate(vector, cosine, sine):
    half_width = vector.shape[-1] // 2
    first_half = vector[:, :half_width]
    second_half = vector[:, half_width:]
    return jnp.concatenate(
        [first_half * cosine - second_half * sine, second_half * cosine + first_half * sine],
        axis=-1,
    )


def total(pair_ref, other_ref):
    quarter = pair_ref.shape[0] // 2
    other = jnp.concatenate([other_ref[quarter:, :], other_ref[:quarter, :]], axis=0)
    return pair_ref[...].astype(F32) + other.astype(F32)


def first_norm(own, beside, gains, layer):
    def body(own_ref, beside_ref, gains_ref, stream_ref, normed_ref):
        stream = jnp.concatenate([own_ref[...], beside_ref[...]], axis=0)
        stream_ref[...] = stream
        normed_ref[...] = norm_forward(stream.astype(F32), gains_ref[0, 0:1, :]).astype(BF16)

    rows, columns = own.shape
    return kernel_call(
        body, [shape(2 * rows, columns, BF16)] * 2, (own, beside, gains), {2: layer}, cost=FORWARD_COST)


def ordered_rows(segments, positions, quarter):
    size = segments.shape[0] // 4

    def body(seg_ref, pos_ref, quarter_ref, across_ref, down_ref):
        lanes = lax.broadcasted_iota(jnp.int32, (1, size), 1)
        lines = [[], [], []]
        for bit in (0, 2, 1, 3):
            index = jnp.bitwise_xor(quarter_ref[0], bit)
            lines[0].append(seg_ref[pl.ds(index, 1), :])
            lines[1].append(lanes + index * size)
            lines[2].append(pos_ref[pl.ds(index, 1), :])
        rows = [jnp.concatenate(line, axis=1).astype(F32) for line in lines]
        across = jnp.concatenate(rows + [jnp.zeros((5, 4 * size), F32)], axis=0)
        across_ref[...] = across
        down_ref[...] = across.T

    return kernel_call(
        body,
        [shape(8, 4 * size, F32), shape(4 * size, 8, F32)],
        (segments.reshape(4, size), positions.reshape(4, size), quarter), cost=FORWARD_COST)


def angles(down, width, theta):
    half_width = width // 2
    frequency = theta ** (-(2.0 * jnp.arange(half_width, dtype=F32)) / width)

    def body(down_ref, frequency_ref, cosine_ref, sine_ref):
        phases = down_ref[:, 2:3] * frequency_ref[...]
        cosine_ref[...] = jnp.cos(phases)
        sine_ref[...] = jnp.sin(phases)

    return tuple(
        kernel_call(
            body,
            [shape(down.shape[0], half_width, F32)] * 2,
            (down, frequency.reshape(1, half_width)), cost=FORWARD_COST)
    )


def after_attention(pair, other, stream, gains, layer):
    def body(pair_ref, other_ref, stream_ref, gains_ref, sum_ref, middle_ref, normed_ref):
        attn_sum = total(pair_ref, other_ref)
        middle = stream_ref[...].astype(F32) + norm_forward(attn_sum, gains_ref[0, 1:2, :])
        sum_ref[...] = attn_sum
        middle_ref[...] = middle
        normed_ref[...] = norm_forward(middle, gains_ref[0, 2:3, :]).astype(BF16)

    size = pair.shape
    return kernel_call(
        body,
        [shape(*size, F32), shape(*size, F32), shape(*size, BF16)],
        (pair, other, stream, gains),
        {3: layer}, cost=FORWARD_COST)


def between_layers(pair, other, middle, gains, layer):
    def body(pair_ref, other_ref, middle_ref, gains_ref, next_ref, sum_ref, result_ref, low_ref):
        mlp_sum = total(pair_ref, other_ref)
        result = middle_ref[...] + norm_forward(mlp_sum, gains_ref[0, 3:4, :])
        sum_ref[...] = mlp_sum
        result_ref[...] = result
        low_ref[...] = norm_forward(result, next_ref[0, 0:1, :]).astype(BF16)

    size = pair.shape
    return kernel_call(
        body,
        [shape(*size, F32), shape(*size, F32), shape(*size, BF16)],
        (pair, other, middle, gains, gains),
        {3: layer, 4: layer + 1}, cost=FORWARD_COST)


def turn_around(pair, other, middle, cotangent, gains, layer):
    def body(pair_ref, other_ref, middle_ref, grad_ref, gains_ref, out_ref, low_ref, gain_ref):
        mlp_sum = total(pair_ref, other_ref)
        gain_row = gains_ref[0, 3:4, :]
        own = out_ref.shape[0]
        result = middle_ref[:own, :] + norm_forward(mlp_sum[:own, :], gain_row)
        out_ref[...] = result.astype(BF16)
        grad, grad_gain = norm_back(mlp_sum, gain_row, grad_ref[...].astype(F32))
        low_ref[...] = grad.astype(BF16)
        gain_ref[...] = grad_gain

    rows, columns = pair.shape
    return kernel_call(
        body,
        [shape(rows // 2, columns, BF16), shape(rows, columns, BF16), shape(1, columns, F32)],
        (pair, other, middle, cotangent, gains),
        {4: layer},
    )


def back_to_attention(pair, other, middle, attn_sum, grad_stream, gains, layer):
    def body(
        pair_ref, other_ref, middle_ref, attn_ref, grad_ref, gains_ref,
        grad_middle_ref, low_ref, gain1_ref, gain2_ref,
    ):
        grad_normed = total(pair_ref, other_ref)
        step, gain2_ref[...] = norm_back(middle_ref[...], gains_ref[0, 2:3, :], grad_normed)
        grad_middle = grad_ref[...].astype(F32) + step
        grad_middle_ref[...] = grad_middle
        grad_attn, gain1_ref[...] = norm_back(attn_ref[...], gains_ref[0, 1:2, :], grad_middle)
        low_ref[...] = grad_attn.astype(BF16)

    rows, columns = pair.shape
    return kernel_call(
        body,
        [shape(rows, columns, F32), shape(rows, columns, BF16)] + [shape(1, columns, F32)] * 2,
        (pair, other, middle, attn_sum, grad_stream, gains),
        {5: layer},
    )


def back_between(pair, other, stream, grad_middle, mlp_sum, gains, layer):
    def body(
        pair_ref, other_ref, stream_ref, grad_ref, mlp_ref, gains_ref, below_ref,
        grad_stream_ref, low_ref, gain0_ref, gain3_ref,
    ):
        grad_normed = total(pair_ref, other_ref)
        step, gain0_ref[...] = norm_back(stream_ref[...], gains_ref[0, 0:1, :], grad_normed)
        grad_stream = grad_ref[...] + step
        grad_stream_ref[...] = grad_stream
        grad_mlp, gain3_ref[...] = norm_back(mlp_ref[...], below_ref[0, 3:4, :], grad_stream)
        low_ref[...] = grad_mlp.astype(BF16)

    rows, columns = pair.shape
    return kernel_call(
        body,
        [shape(rows, columns, F32), shape(rows, columns, BF16)] + [shape(1, columns, F32)] * 2,
        (pair, other, stream, grad_middle, mlp_sum, gains, gains),
        {5: layer, 6: layer - 1},
    )


def back_to_input(pair, other, stream, grad_middle, gains, layer):
    def body(pair_ref, other_ref, stream_ref, grad_ref, gains_ref, out_ref):
        own = out_ref.shape[0]
        grad_normed = pair_ref[:own, :].astype(F32) + other_ref[own:, :].astype(F32)
        step, unused = norm_back(
            stream_ref[:own, :].astype(F32), gains_ref[0, 0:1, :], grad_normed
        )
        out_ref[...] = (grad_ref[:own, :] + step).astype(BF16)

    rows, columns = pair.shape
    return kernel_call(
        body,
        [shape(rows // 2, columns, BF16)],
        (pair, other, stream, grad_middle, gains),
        {4: layer},
    )[0]


def allowed_rows(down_ref, across_ref, start, count, window):
    seg_down = down_ref[start : start + count, 0:1]
    place_down = down_ref[start : start + count, 1:2]
    seg_across = across_ref[0:1, :]
    place_across = across_ref[1:2, :]
    allowed = (seg_down == seg_across) & (place_across <= place_down)
    if window < SEQ_LEN:
        allowed = allowed & (place_down - place_across < window)
    return allowed


def attention(own, received, weights, tables, layer, window):
    w_query, w_key, w_value, w_out, qk_gains = weights
    cosine, sine, down, across = tables
    half = own.shape[0]
    length = 2 * half
    head_width = w_key.shape[2]

    def body(
        own_ref, received_ref, wq_ref, wk_ref, wv_ref, wo_ref, gain_ref,
        cos_ref, sin_ref, down_ref, across_ref,
        kept_ref, sent_ref, qraw_ref, kraw_ref, q_ref, k_ref, v_ref, attended_ref, lse_ref,
    ):
        for part, source in ((0, own_ref), (1, received_ref)):
            rows = slice(part * half, (part + 1) * half)
            normed = source[...]
            cos_rows, sin_rows = cos_ref[rows, :], sin_ref[rows, :]
            key_raw = product(normed, wk_ref[0])
            kraw_ref[rows, :] = key_raw
            k_ref[rows, :] = rotate(
                norm_forward(key_raw, gain_ref[0, 1:2, :]), cos_rows, sin_rows
            ).astype(BF16)
            v_ref[rows, :] = product(normed, wv_ref[0]).astype(BF16)
            query_raw = product(normed, wq_ref[0])
            qraw_ref[rows, :] = query_raw
            q_ref[rows, :] = rotate(
                norm_forward(query_raw, gain_ref[0, 0:1, :]), cos_rows, sin_rows
            ).astype(BF16)
        for part, target in ((1, sent_ref), (0, kept_ref)):
            rows = slice(part * half, (part + 1) * half)
            scores = product_right(q_ref[rows, :], k_ref[...]) * score_scale
            allowed = allowed_rows(down_ref, across_ref, part * half, half, window)
            masked = jnp.where(allowed, scores, masked_fill)
            row_max = jnp.max(masked, axis=-1, keepdims=True)
            expo = jnp.where(allowed, jnp.exp(masked - row_max), 0.0)
            row_sum = jnp.sum(expo, axis=-1, keepdims=True)
            probability = (expo * (1.0 / row_sum)).astype(BF16)
            lse_ref[rows, :] = row_max + jnp.log(row_sum)
            attended = product(probability, v_ref[...]).astype(BF16)
            attended_ref[rows, :] = attended
            target[...] = product(attended, wo_ref[0]).astype(BF16)

    width = own.shape[1]
    return kernel_call(
        body,
        [shape(half, width, BF16)] * 2
        + [shape(length, head_width, F32)] * 2
        + [shape(length, head_width, BF16)] * 4
        + [shape(length, 1, F32)],
        (own, received, w_query, w_key, w_value, w_out, qk_gains, cosine, sine, down, across),
        {place: layer for place in (2, 3, 4, 5, 6)}, cost=FORWARD_COST)


def feed_forward(own, received, weights, layer):
    half, width = own.shape
    w_gate, w_up, w_down = weights
    hidden_width = w_gate.shape[2]
    length = 2 * half

    def body(own_ref, received_ref, wg_ref, wu_ref, wd_ref, kept_ref, sent_ref, g_ref, u_ref, h_ref):
        for part, source, target in ((1, received_ref, sent_ref), (0, own_ref, kept_ref)):
            rows = slice(part * half, (part + 1) * half)
            normed = source[...]
            gate = product(normed, wg_ref[0])
            up = product(normed, wu_ref[0])
            g_ref[rows, :] = gate
            u_ref[rows, :] = up
            bend = jnp.tanh(gelu_slope * (gate + gelu_cubic * (gate * gate * gate)))
            hidden = (gate * (0.5 * (1.0 + bend)) * up).astype(BF16)
            h_ref[rows, :] = hidden
            target[...] = product(hidden, wd_ref[0]).astype(BF16)

    return kernel_call(
        body,
        [shape(half, width, BF16)] * 2
        + [shape(length, hidden_width, F32)] * 2
        + [shape(length, hidden_width, BF16)],
        (own, received, w_gate, w_up, w_down),
        {2: layer, 3: layer, 4: layer}, cost=FORWARD_COST)


def feed_forward_back(own, received, weights, gate, up, layer):
    half, width = own.shape
    w_gate, w_up, w_down = weights
    hidden_width = w_gate.shape[2]
    length = 2 * half

    def body(
        own_ref, received_ref, wg_ref, wu_ref, wd_ref, g_ref, u_ref,
        kept_ref, sent_ref, gate_low_ref, up_low_ref,
    ):
        for part, source, target in ((1, received_ref, sent_ref), (0, own_ref, kept_ref)):
            rows = slice(part * half, (part + 1) * half)
            grad_hidden = product_right(source[...], wd_ref[0])
            gate_in = g_ref[rows, :]
            square = gate_in * gate_in
            bend = jnp.tanh(gelu_slope * gate_in * (1.0 + gelu_cubic * square))
            lift = 0.5 * (1.0 + bend)
            slope = lift + 0.5 * gate_in * (1.0 - bend * bend) * (
                gelu_slope * (1.0 + 3.0 * gelu_cubic * square)
            )
            gate_low = (grad_hidden * u_ref[rows, :] * slope).astype(BF16)
            up_low = (grad_hidden * (gate_in * lift)).astype(BF16)
            gate_low_ref[rows, :] = gate_low
            up_low_ref[rows, :] = up_low
            target[...] = (
                product_right(gate_low, wg_ref[0]) + product_right(up_low, wu_ref[0])
            ).astype(BF16)

    return kernel_call(
        body,
        [shape(half, width, BF16)] * 2 + [shape(length, hidden_width, BF16)] * 2,
        (own, received, w_gate, w_up, w_down, gate, up),
        {2: layer, 3: layer, 4: layer},
    )


def attention_back(own, received, weights, tables, saved, side, layer, window, first=()):
    w_query, w_key, w_value, w_out, qk_gains = weights
    cosine, sine, down, across = tables
    query_raw, key_raw, queries, key_rows, values, row_lse = saved
    half, width = own.shape
    length = 2 * half
    head_width = w_key.shape[2]

    def body(
        own_ref, received_ref, wq_ref, wk_ref, wv_ref, wo_ref, gain_ref,
        cos_ref, sin_ref, down_ref, across_ref,
        qraw_ref, kraw_ref, q_ref, k_ref, v_ref, lse_ref, side_ref,
        *rest,
    ):
        firsts, rest = rest[: len(first)], rest[len(first) :]
        kept_ref, sent_ref, gq_ref, mine_ref, theirs_ref, qgain_ref, kgain_ref = rest[:7]
        *gain0_refs, gk_ref, gv_ref = rest[7:]
        grad_keys = None
        grad_values = None
        query_gain = None
        for part, source in ((0, own_ref), (1, received_ref)):
            rows = slice(part * half, (part + 1) * half)
            grad_attended = product_right(source[...], wo_ref[0]).astype(BF16)
            queries_part = q_ref[rows, :]
            scores = product_right(queries_part, k_ref[...]) * score_scale
            allowed = allowed_rows(down_ref, across_ref, part * half, half, window)
            probability = jnp.where(allowed, jnp.exp(scores - lse_ref[rows, :]), 0.0)
            values_term = product_left(probability.astype(BF16), grad_attended)
            grad_prob = product_right(grad_attended, v_ref[...])
            inner_sum = jnp.sum(probability * grad_prob, axis=-1, keepdims=True)
            grad_scores = (probability * (grad_prob - inner_sum)).astype(BF16)
            keys_term = product_left(grad_scores, queries_part)
            grad_values = values_term if grad_values is None else grad_values + values_term
            grad_keys = keys_term if grad_keys is None else grad_keys + keys_term
            grad_queries = (product(grad_scores, k_ref[...]) * score_scale).astype(BF16)
            turned = rotate(grad_queries.astype(F32), cos_ref[rows, :], -sin_ref[rows, :])
            grad_raw, gain_term = norm_back(qraw_ref[rows, :], gain_ref[0, 0:1, :], turned)
            query_gain = gain_term if query_gain is None else query_gain + gain_term
            gq_ref[rows, :] = grad_raw.astype(BF16)
        qgain_ref[...] = query_gain
        grad_keys = (grad_keys * score_scale).astype(BF16)
        turned = rotate(grad_keys.astype(F32), cos_ref[...], -sin_ref[...])
        grad_raw, kgain_ref[...] = norm_back(kraw_ref[...], gain_ref[0, 1:2, :], turned)
        gk_ref[...] = grad_raw.astype(BF16)
        gv_ref[...] = grad_values.astype(BF16)

        @pl.when(side_ref[0] == 0)
        def keys_here():
            mine_ref[...] = gk_ref[...]
            theirs_ref[...] = gv_ref[...]

        @pl.when(side_ref[0] != 0)
        def values_here():
            mine_ref[...] = gv_ref[...]
            theirs_ref[...] = gk_ref[...]

        for part, target in ((1, sent_ref), (0, kept_ref)):
            rows = slice(part * half, (part + 1) * half)
            target[...] = (
                product_right(gq_ref[rows, :], wq_ref[0])
                + product_right(gk_ref[rows, :], wk_ref[0])
                + product_right(gv_ref[rows, :], wv_ref[0])
            ).astype(BF16)
        if first:
            low_ref, other_ref, norm_ref = firsts
            gain0_refs[0][...] = (
                jnp.sum(
                    kept_ref[...].astype(F32) * low_ref[...].astype(F32)
                    + sent_ref[...].astype(F32) * other_ref[...].astype(F32),
                    axis=0,
                    keepdims=True,
                )
                / norm_ref[0, 0:1, :]
            )

    fixed = {place: layer for place in (2, 3, 4, 5, 6)}
    if first:
        fixed[20] = layer
    return kernel_call(
        body,
        [shape(half, width, BF16)] * 2
        + [shape(length, head_width, BF16)] * 3
        + [shape(1, head_width, F32)] * 2
        + [shape(1, width, F32)] * (1 if first else 0),
        (
            own, received, w_query, w_key, w_value, w_out, qk_gains,
            cosine, sine, down, across, query_raw, key_raw, queries, key_rows, values, row_lse, side,
            *first,
        ),
        fixed,
        scratch=[pltpu.VMEM((length, head_width), BF16)] * 2,
    )


def slot_masks(bits):
    count = len(bits)
    return [
        sum(bit for place, bit in enumerate(bits) if slot >> (count - 1 - place) & 1)
        for slot in range(1 << count)
    ]


def gradient_blocks(factors, me, bits, gains=()):
    pieces = 1 << len(bits)
    masks = slot_masks(bits)
    sizes = [(l[0].shape[1] // pieces, r[0].shape[1] // LANES) for l, r in factors]
    rows = sum(tall * wide for tall, wide in sizes)
    if any(tall % 16 for tall, wide in sizes):
        chunks = me[0] ^ jnp.array(masks, jnp.int32)
        parts = []
        for (left, right), (tall, wide) in zip(factors, sizes):
            grad = product_left(jnp.concatenate(left), jnp.concatenate(right)).astype(BF16)
            cut = grad.reshape(pieces, tall, wide, LANES).transpose(0, 2, 1, 3)
            parts.append(cut.reshape(pieces, tall * wide, LANES))
        if gains:
            rows = [
                jnp.pad(row.reshape(pieces, 1, -1), ((0, 0), (0, 0), (0, LANES - row.shape[1] // pieces)))
                for row in gains
            ]
            block = jnp.concatenate(rows, axis=1)
            parts.append(
                jnp.pad(block, ((0, 0), (0, GAIN_ROWS - len(rows)), (0, 0))).astype(BF16)
            )
        blocks = jnp.take(jnp.concatenate(parts, axis=1), chunks, axis=0)
        return (blocks[: pieces // 2], blocks[pieces // 2 :])
    flat = []
    where = []
    for pair in factors:
        places = []
        for side in pair:
            places.append(list(range(len(flat), len(flat) + len(side))))
            flat.extend(side)
        where.append(places)

    def body(*refs):
        me_ref, inputs = refs[0], refs[1 : 1 + len(flat)]
        gain_refs = refs[1 + len(flat) : 1 + len(flat) + len(gains)]
        kept_ref, sent_ref, *scratch = refs[1 + len(flat) + len(gains) :]
        base = 0
        for (lefts, rights), (tall, wide), held in zip(where, sizes, scratch):
            def side(places):
                arrays = [inputs[place][...] for place in places]
                return arrays[0] if len(arrays) == 1 else jnp.concatenate(arrays, axis=0)

            held[...] = product_left(side(lefts), side(rights))
            for slot, mask in enumerate(masks):
                chunk = jnp.bitwise_xor(me_ref[0], mask)
                start = pl.multiple_of(chunk * tall, tall)
                target = kept_ref if slot < pieces // 2 else sent_ref
                block = held[pl.ds(start, tall), :].astype(BF16)
                for column in range(wide):
                    low = base + column * tall
                    target[slot % (pieces // 2), low : low + tall, :] = block[
                        :, column * LANES : (column + 1) * LANES
                    ]
            base += tall * wide
        if gains:
            table = scratch[-1]
            table[...] = jnp.zeros_like(table)
            for place, ref in enumerate(gain_refs):
                count = ref.shape[1] // pieces
                for chunk in range(pieces):
                    line = chunk * GAIN_ROWS + place
                    table[line : line + 1, :count] = ref[:, chunk * count : (chunk + 1) * count]
            for slot, mask in enumerate(masks):
                chunk = jnp.bitwise_xor(me_ref[0], mask)
                start = pl.multiple_of(chunk * GAIN_ROWS, GAIN_ROWS)
                target = kept_ref if slot < pieces // 2 else sent_ref
                target[slot % (pieces // 2), base : base + GAIN_ROWS, :] = table[
                    pl.ds(start, GAIN_ROWS), :
                ].astype(BF16)

    rows += GAIN_ROWS if gains else 0
    out = jax.ShapeDtypeStruct((pieces // 2, rows, LANES), BF16)
    args = (me, *flat, *gains)
    specs = [pl.BlockSpec(memory_space=pltpu.SMEM)] + [
        pl.BlockSpec(a.shape, lambda i: (0, 0)) for a in args[1:]
    ]
    return pl.pallas_call(
        body,
        grid=(1,),
        in_specs=specs,
        out_specs=[pl.BlockSpec(out.shape, lambda i: (0, 0, 0))] * 2,
        out_shape=[out, out],
        scratch_shapes=[
            pltpu.VMEM((tall * pieces, wide * LANES), F32) for tall, wide in sizes
        ]
        + [pltpu.VMEM((pieces * GAIN_ROWS, LANES), F32)] * (1 if gains else 0),
        compiler_params=pltpu.CompilerParams(vmem_limit_bytes=VMEM_BYTES),
        cost_estimate=pl.CostEstimate(flops=1, transcendentals=0, bytes_accessed=1),
    )(*args)


def after(gate, *values):
    return lax.optimization_barrier((gate,) + values)[1:]


class Halving:
    def __init__(self, terms, me, bits, gains=()):
        self.kept, sent = gradient_blocks(terms, me, bits, gains)
        self.bits = bits
        self.arrived = swap(sent, "dp", bits[0])

    def step(self, gate=None):
        if not self.bits:
            return
        kept, arrived = self.kept, self.arrived
        if gate is not None:
            kept, arrived = after(gate, kept, arrived)
        self.bits = self.bits[1:]
        if self.bits:
            middle = kept.shape[0] // 2
            sent = (kept[middle:].astype(F32) + arrived[middle:].astype(F32)).astype(BF16)
            self.arrived = swap(sent, "dp", self.bits[0])
            self.kept = kept[:middle].astype(F32) + arrived[:middle].astype(F32)
        else:
            self.kept = kept[0].astype(F32) + arrived[0].astype(F32)

    def finish(self):
        while self.bits:
            self.step()
        return self.kept


def assembled(sources, layout, sizes, exchanged, starts, shared_size, gains_at, gain_widths):
    sizes = sizes + [shared_size] * 2
    here, there, side = exchanged
    outs = [jax.ShapeDtypeStruct((2, tall, columns), F32) for tall, columns in sizes]
    outs += [
        jax.ShapeDtypeStruct((2, 4, gain_widths[0]), F32),
        jax.ShapeDtypeStruct((2, 2, gain_widths[1]), F32),
    ]

    if any(tall % 16 for tall, columns in sizes):

        def joined(array, start, tall, columns):
            return jnp.concatenate(
                [
                    array[start + place * tall : start + (place + 1) * tall]
                    for place in range(columns // LANES)
                ],
                axis=1,
            ).astype(F32)

        results = [
            jnp.stack([joined(sources[source], start, *size) for source, start in both])
            for both, size in zip(layout, sizes)
        ]
        for first, second in ((here, there), (there, here)):
            picked = jnp.where(side == 0, first, second)
            results.append(jnp.stack([joined(picked, start, *shared_size) for start in starts]))
        gains = here[gains_at : gains_at + GAIN_ROWS].astype(F32)
        gains = (gains + there[gains_at : gains_at + GAIN_ROWS].astype(F32))[:12]
        gains = gains.reshape(2, 6, LANES)
        return results + [gains[:, :4, : gain_widths[0]], gains[:, 4:, : gain_widths[1]]]

    def body(*refs):
        inputs = refs[: len(sources)]
        here_ref, there_ref, side_ref = refs[len(sources) : len(sources) + 3]
        *targets, norm_ref, qk_ref = refs[len(sources) + 3 :]

        def put(target, layer, source, start, tall, columns):
            for column in range(columns // LANES):
                low = start + column * tall
                target[layer, :, column * LANES : (column + 1) * LANES] = source[
                    low : low + tall, :
                ].astype(F32)

        for member, both in enumerate(layout):
            for layer, (source, start) in enumerate(both):
                put(targets[member], layer, inputs[source], start, *sizes[member])
        key_ref, value_ref = targets[-2:]

        @pl.when(side_ref[0] == 0)
        def keys_here():
            for layer, start in enumerate(starts):
                put(key_ref, layer, here_ref, start, *shared_size)
                put(value_ref, layer, there_ref, start, *shared_size)

        @pl.when(side_ref[0] != 0)
        def values_here():
            for layer, start in enumerate(starts):
                put(key_ref, layer, there_ref, start, *shared_size)
                put(value_ref, layer, here_ref, start, *shared_size)

        gains = here_ref[gains_at : gains_at + GAIN_ROWS, :].astype(F32)
        gains = gains + there_ref[gains_at : gains_at + GAIN_ROWS, :].astype(F32)
        for layer in range(2):
            norm_ref[layer] = gains[6 * layer : 6 * layer + 4, : gain_widths[0]]
            qk_ref[layer] = gains[6 * layer + 4 : 6 * layer + 6, : gain_widths[1]]

    return kernel_call(body, outs, (*sources, here, there, side))


def local(
    hidden_in,
    cotangent,
    segments,
    positions,
    w_query,
    w_key,
    w_value,
    w_out,
    w_gate,
    w_up,
    w_down,
    norm_gains,
    qk_gains,
):
    head_width = w_key.shape[2]
    windows = (WINDOW, SEQ_LEN)
    pieces = lax.axis_size("dp")
    quarter = lax.axis_index("tensor")
    me = lax.axis_index("dp").astype(jnp.int32).reshape(1)
    side = jnp.bitwise_and(quarter, 1).astype(jnp.int32).reshape(1)
    hidden_in, segments, positions, quarter, me, side = lax.optimization_barrier(
        (hidden_in, segments, positions, quarter, me, side)
    )
    bits = [1 << place for place in range(pieces.bit_length() - 1)]
    mlp1_bits = [bits[p] for p in [0, 1, 2]] + bits[3:] if len(bits) > 2 else bits
    attn1_bits = [bits[p] for p in [0, 1, 2]] + bits[3:] if len(bits) > 2 else bits
    mlp0_bits = [bits[p] for p in [0, 1, 2]] + bits[3:] if len(bits) > 2 else bits
    attn0_bits = [bits[p] for p in [1, 0, 2]] + bits[3:] if len(bits) > 2 else bits
    across, down = ordered_rows(segments, positions, quarter.reshape(1))
    attn_weights = (w_query, w_key, w_value, w_out, qk_gains)
    mlp_weights = (w_gate, w_up, w_down)
    tables = [angles(down, head_width, thetas[0]) + (down, across), None]

    beside = swap(hidden_in, "tensor", 2)
    (beside,) = after(tables[0], beside)
    stream, low = first_norm(hidden_in, beside, norm_gains, 0)
    saved = []
    for layer in range(2):
        received = swap(low, "tensor", 1)
        kept, sent, *kept_attn = attention(
            low, received, attn_weights, tables[layer], layer, windows[layer]
        )
        attn_in = (low, received)
        pair, other = summed_pair(kept, sent)
        if layer == 0:
            (rows,) = after(pair, down)
            tables[1] = angles(rows, head_width, thetas[1]) + (down, across)
            (other,) = after(tables[1], other)
        attn_sum, middle, low = after_attention(pair, other, stream, norm_gains, layer)
        received = swap(low, "tensor", 1)
        kept, sent, *kept_mlp = feed_forward(low, received, mlp_weights, layer)
        mlp_in = (low, received)
        pair, other = summed_pair(kept, sent)
        saved.append([attn_in, kept_attn, attn_sum, middle, mlp_in, kept_mlp, stream])
        if layer == 0:
            mlp_sum, stream, low = between_layers(pair, other, middle, norm_gains, layer)

    grad_stream = jnp.concatenate([cotangent, swap(cotangent, "tensor", 2)])
    output, low, gain3 = turn_around(pair, other, middle, grad_stream, norm_gains, 1)
    sums = {}
    gain_rows = [None, None]
    for layer in (1, 0):
        attn_in, kept_attn, attn_sum, middle, mlp_in, kept_mlp, stream = saved[layer]
        gate, up, hidden = kept_mlp
        query_raw, key_raw, queries, key_rows, values, attended, row_lse = kept_attn
        received = swap(low, "tensor", 1)
        kept, sent, gate_low, up_low = feed_forward_back(
            low, received, mlp_weights, gate, up, layer
        )
        mlp_out = (low, received)
        if layer == 0:
            sums["attn1"].step(gate_low)
            (kept,) = after(sums["attn1"].kept, kept)
        pair, other = summed_pair(kept, sent)
        gate_low, up_low = after(pair, gate_low, up_low)
        gate_term, up_term = (mlp_in, (gate_low,)), (mlp_in, (up_low,))
        down_term = ((hidden,), mlp_out)
        if layer == 1:
            sums["mlp1"] = Halving([gate_term, up_term, down_term], me, mlp1_bits)
            (other,) = after(sums["mlp1"].kept, other)
        else:
            sums["mlp0"] = Halving([gate_term, up_term, down_term], me, mlp0_bits)
            sums["mlp1"].step((sums["mlp0"].kept, other))
            (other,) = after([s.kept for s in sums.values()], other)
        grad_middle, low, gain1, gain2 = back_to_attention(
            pair, other, middle, attn_sum, grad_stream, norm_gains, layer
        )
        received = swap(low, "tensor", 1)
        kept, sent, grad_q, mine, theirs, gain_q, gain_k, *gain0 = attention_back(
            low,
            received,
            attn_weights,
            tables[layer],
            (query_raw, key_raw, queries, key_rows, values, row_lse),
            side,
            layer,
            windows[layer],
            () if layer else (*attn_in, norm_gains),
        )
        pair, other = summed_pair(kept, sent)
        theirs = swap(theirs, "tensor", 1)
        if layer == 1:
            grad_q, mine, theirs = after(pair, grad_q, mine, theirs)
        shared_term = (attn_in + attn_in[::-1], (mine, theirs))
        query_term, out_term = (attn_in, (grad_q,)), ((attended,), (low, received))
        gain_rows[layer] = [None, gain1 * 0.5, gain2 * 0.5, gain3 * 0.5, gain_q, gain_k]
        if layer == 1:
            sums["attn1"] = Halving([query_term, out_term, shared_term], me, attn1_bits)
            sums["mlp1"].step(sums["attn1"].kept)
            (other,) = after([s.kept for s in sums.values()], other)
            grad_stream, low, gain0, gain3 = back_between(
                pair, other, stream, grad_middle, mlp_sum, norm_gains, layer
            )
            gain_rows[1][0] = gain0 * 0.5
        else:
            gain_rows[0][0] = gain0[0]
            sums["attn0"] = Halving(
                [query_term, out_term, shared_term],
                me,
                attn0_bits,
                gain_rows[0] + gain_rows[1],
            )
            grad_input = back_to_input(pair, other, stream, grad_middle, norm_gains, layer)

    sums["mlp1"].step(sums["attn0"].kept)
    sums["attn1"].step(sums["attn0"].kept)
    sums["mlp0"].step(sums["attn0"].kept)
    sums["attn0"].step(sums["mlp0"].kept)
    sums["attn0"].step()
    sums["mlp0"].step(sums["attn0"].kept)
    sums["attn0"].finish()

    tall = {
        "q": w_query.shape[1] // pieces,
        "o": w_out.shape[1] // pieces,
        "g": w_gate.shape[1] // pieces,
        "d": w_down.shape[1] // pieces,
    }
    heads_rows = tall["q"] * head_width // LANES
    gate_rows = tall["g"] * w_gate.shape[2] // LANES
    both_rows = heads_rows + tall["o"] * w_out.shape[2] // LANES
    done = {name: halving.finish() for name, halving in sums.items()}
    low = jnp.concatenate([done["attn0"][both_rows:], done["attn1"][both_rows:]]).astype(BF16)
    here = (low.astype(F32) + swap(low, "tensor", 2).astype(F32)).astype(BF16)
    there = swap(here, "tensor", 1)
    first_rows = done["attn0"].shape[0] - both_rows
    *grads, grad_norm_gains, grad_qk_gains = assembled(
        [done[name] for name in ("attn0", "attn1", "mlp0", "mlp1")],
        [
            [(0, 0), (1, 0)],
            [(0, heads_rows), (1, heads_rows)],
            [(2, 0), (3, 0)],
            [(2, gate_rows), (3, gate_rows)],
            [(2, 2 * gate_rows), (3, 2 * gate_rows)],
        ],
        [(tall["q"], head_width), (tall["o"], w_out.shape[2])]
        + [(tall["g"], w_gate.shape[2])] * 2
        + [(tall["d"], w_down.shape[2])],
        (here, there, side),
        [0, first_rows],
        (tall["q"], head_width),
        first_rows - GAIN_ROWS,
        (norm_gains.shape[2] // pieces, head_width // pieces),
    )
    grad_query, grad_out, grad_gate, grad_up, grad_down, grad_key, grad_value = grads
    return (
        output,
        grad_input,
        grad_query,
        grad_key,
        grad_value,
        grad_out,
        grad_gate,
        grad_up,
        grad_down,
        grad_norm_gains,
        grad_qk_gains,
    )


def solution(mesh):
    return jax.shard_map(
        local,
        mesh=mesh,
        in_specs=(
            P(("dp", "tensor"), None),
            P(("dp", "tensor"), None),
            P("dp"),
            P("dp"),
            P(None, None, "tensor"),
            P(),
            P(),
            P(None, "tensor", None),
            P(None, None, "tensor"),
            P(None, None, "tensor"),
            P(None, "tensor", None),
            P(),
            P(),
        ),
        out_specs=(
            P(("dp", "tensor"), None),
            P(("dp", "tensor"), None),
            P(None, "dp", "tensor"),
            P(None, "dp", None),
            P(None, "dp", None),
            P(None, ("tensor", "dp"), None),
            P(None, "dp", "tensor"),
            P(None, "dp", "tensor"),
            P(None, ("tensor", "dp"), None),
            P(None, None, "dp"),
            P(None, None, "dp"),
        ),
        check_vma=False,
    )
```

```python
import jax
import jax.numpy as jnp
from jax import lax
from jax.experimental import pallas as pl
from jax.experimental.pallas import tpu as pltpu
from jax.sharding import PartitionSpec as P

WINDOW = 512
SEQ_LEN = 512
LANES = 128
VMEM_BYTES = 12 << 20
FORWARD_COST = (1_000_000_000, 4_000_000)
GAIN_ROWS = 16

epsilon = 1e-06
score_scale = 0.0625
masked_fill = -1e30
thetas = (10000.0, 1000000.0)
gelu_slope = 0.7978845608028654
gelu_cubic = 0.044715

F32 = jnp.float32
BF16 = jnp.bfloat16


def product(left, right):
    return jnp.dot(left, right, preferred_element_type=F32)


def product_left(left, right):
    return lax.dot_general(left, right, (((0,), (0,)), ((), ())), preferred_element_type=F32)


def product_right(left, right):
    return lax.dot_general(left, right, (((1,), (1,)), ((), ())), preferred_element_type=F32)


def swap(array, axis, bit):
    size = lax.axis_size(axis)
    return lax.ppermute(array, axis, [(i, i ^ bit) for i in range(size)])


def summed_pair(kept, sent):
    pair = (kept.astype(F32) + swap(sent, "tensor", 1).astype(F32)).astype(BF16)
    return (pair, swap(pair, "tensor", 2))


def kernel_call(body, outs, args, layers=None, scratch=(), cost=(1, 1)):
    layers = layers or {}

    def spec(place, arg):
        if place in layers:
            rest = arg.shape[1:]
            fixed = (layers[place],) + (0,) * len(rest)
            return pl.BlockSpec((1,) + rest, lambda i, fixed=fixed: fixed)
        if arg.shape == (1,):
            return pl.BlockSpec(memory_space=pltpu.SMEM)
        return pl.BlockSpec(arg.shape, lambda i, n=arg.ndim: (0,) * n)

    return pl.pallas_call(
        body,
        grid=(1,),
        in_specs=[spec(place, arg) for place, arg in enumerate(args)],
        out_specs=[pl.BlockSpec(o.shape, lambda i, n=len(o.shape): (0,) * n) for o in outs],
        out_shape=list(outs),
        scratch_shapes=list(scratch),
        compiler_params=pltpu.CompilerParams(vmem_limit_bytes=VMEM_BYTES),
        cost_estimate=pl.CostEstimate(
            flops=cost[0], transcendentals=0, bytes_accessed=cost[1]
        ),
    )(*args)


def shape(rows, columns, dtype):
    return jax.ShapeDtypeStruct((rows, columns), dtype)


def inverse_rms(vector):
    return lax.rsqrt(jnp.mean(vector * vector, axis=-1, keepdims=True) + epsilon)


def norm_forward(vector, gain_row):
    return vector * inverse_rms(vector) * gain_row


def norm_back(vector, gain_row, grad_out):
    scale = inverse_rms(vector)
    scaled = grad_out * gain_row
    inner = jnp.mean(scaled * vector, axis=-1, keepdims=True)
    grad = scale * scaled - vector * (scale * scale * scale * inner)
    grad_gain = jnp.sum(grad_out * (vector * scale), axis=0, keepdims=True)
    return (grad, grad_gain)


def rotate(vector, cosine, sine):
    half_width = vector.shape[-1] // 2
    first_half = vector[:, :half_width]
    second_half = vector[:, half_width:]
    return jnp.concatenate(
        [first_half * cosine - second_half * sine, second_half * cosine + first_half * sine],
        axis=-1,
    )


def total(pair_ref, other_ref):
    quarter = pair_ref.shape[0] // 2
    other = jnp.concatenate([other_ref[quarter:, :], other_ref[:quarter, :]], axis=0)
    return pair_ref[...].astype(F32) + other.astype(F32)


def first_norm(own, beside, gains, layer):
    def body(own_ref, beside_ref, gains_ref, stream_ref, normed_ref):
        stream = jnp.concatenate([own_ref[...], beside_ref[...]], axis=0)
        stream_ref[...] = stream
        normed_ref[...] = norm_forward(stream.astype(F32), gains_ref[0, 0:1, :]).astype(BF16)

    rows, columns = own.shape
    return kernel_call(
        body, [shape(2 * rows, columns, BF16)] * 2, (own, beside, gains), {2: layer}, cost=FORWARD_COST)


def ordered_rows(segments, positions, quarter):
    size = segments.shape[0] // 4

    def body(seg_ref, pos_ref, quarter_ref, across_ref, down_ref):
        lanes = lax.broadcasted_iota(jnp.int32, (1, size), 1)
        lines = [[], [], []]
        for bit in (0, 2, 1, 3):
            index = jnp.bitwise_xor(quarter_ref[0], bit)
            lines[0].append(seg_ref[pl.ds(index, 1), :])
            lines[1].append(lanes + index * size)
            lines[2].append(pos_ref[pl.ds(index, 1), :])
        rows = [jnp.concatenate(line, axis=1).astype(F32) for line in lines]
        across = jnp.concatenate(rows + [jnp.zeros((5, 4 * size), F32)], axis=0)
        across_ref[...] = across
        down_ref[...] = across.T

    return kernel_call(
        body,
        [shape(8, 4 * size, F32), shape(4 * size, 8, F32)],
        (segments.reshape(4, size), positions.reshape(4, size), quarter), cost=FORWARD_COST)


def angles(down, width, theta):
    half_width = width // 2
    frequency = theta ** (-(2.0 * jnp.arange(half_width, dtype=F32)) / width)

    def body(down_ref, frequency_ref, cosine_ref, sine_ref):
        phases = down_ref[:, 2:3] * frequency_ref[...]
        cosine_ref[...] = jnp.cos(phases)
        sine_ref[...] = jnp.sin(phases)

    return tuple(
        kernel_call(
            body,
            [shape(down.shape[0], half_width, F32)] * 2,
            (down, frequency.reshape(1, half_width)), cost=FORWARD_COST)
    )


def after_attention(pair, other, stream, gains, layer):
    def body(pair_ref, other_ref, stream_ref, gains_ref, sum_ref, middle_ref, normed_ref):
        attn_sum = total(pair_ref, other_ref)
        middle = stream_ref[...].astype(F32) + norm_forward(attn_sum, gains_ref[0, 1:2, :])
        sum_ref[...] = attn_sum
        middle_ref[...] = middle
        normed_ref[...] = norm_forward(middle, gains_ref[0, 2:3, :]).astype(BF16)

    size = pair.shape
    return kernel_call(
        body,
        [shape(*size, F32), shape(*size, F32), shape(*size, BF16)],
        (pair, other, stream, gains),
        {3: layer}, cost=FORWARD_COST)


def between_layers(pair, other, middle, gains, layer):
    def body(pair_ref, other_ref, middle_ref, gains_ref, next_ref, sum_ref, result_ref, low_ref):
        mlp_sum = total(pair_ref, other_ref)
        result = middle_ref[...] + norm_forward(mlp_sum, gains_ref[0, 3:4, :])
        sum_ref[...] = mlp_sum
        result_ref[...] = result
        low_ref[...] = norm_forward(result, next_ref[0, 0:1, :]).astype(BF16)

    size = pair.shape
    return kernel_call(
        body,
        [shape(*size, F32), shape(*size, F32), shape(*size, BF16)],
        (pair, other, middle, gains, gains),
        {3: layer, 4: layer + 1}, cost=FORWARD_COST)


def turn_around(pair, other, middle, cotangent, gains, layer):
    def body(pair_ref, other_ref, middle_ref, grad_ref, gains_ref, out_ref, low_ref, gain_ref):
        mlp_sum = total(pair_ref, other_ref)
        gain_row = gains_ref[0, 3:4, :]
        own = out_ref.shape[0]
        result = middle_ref[:own, :] + norm_forward(mlp_sum[:own, :], gain_row)
        out_ref[...] = result.astype(BF16)
        grad, grad_gain = norm_back(mlp_sum, gain_row, grad_ref[...].astype(F32))
        low_ref[...] = grad.astype(BF16)
        gain_ref[...] = grad_gain

    rows, columns = pair.shape
    return kernel_call(
        body,
        [shape(rows // 2, columns, BF16), shape(rows, columns, BF16), shape(1, columns, F32)],
        (pair, other, middle, cotangent, gains),
        {4: layer},
    )


def back_to_attention(pair, other, middle, attn_sum, grad_stream, gains, layer):
    def body(
        pair_ref, other_ref, middle_ref, attn_ref, grad_ref, gains_ref,
        grad_middle_ref, low_ref, gain1_ref, gain2_ref,
    ):
        grad_normed = total(pair_ref, other_ref)
        step, gain2_ref[...] = norm_back(middle_ref[...], gains_ref[0, 2:3, :], grad_normed)
        grad_middle = grad_ref[...].astype(F32) + step
        grad_middle_ref[...] = grad_middle
        grad_attn, gain1_ref[...] = norm_back(attn_ref[...], gains_ref[0, 1:2, :], grad_middle)
        low_ref[...] = grad_attn.astype(BF16)

    rows, columns = pair.shape
    return kernel_call(
        body,
        [shape(rows, columns, F32), shape(rows, columns, BF16)] + [shape(1, columns, F32)] * 2,
        (pair, other, middle, attn_sum, grad_stream, gains),
        {5: layer},
    )


def back_between(pair, other, stream, grad_middle, mlp_sum, gains, layer):
    def body(
        pair_ref, other_ref, stream_ref, grad_ref, mlp_ref, gains_ref, below_ref,
        grad_stream_ref, low_ref, gain0_ref, gain3_ref,
    ):
        grad_normed = total(pair_ref, other_ref)
        step, gain0_ref[...] = norm_back(stream_ref[...], gains_ref[0, 0:1, :], grad_normed)
        grad_stream = grad_ref[...] + step
        grad_stream_ref[...] = grad_stream
        grad_mlp, gain3_ref[...] = norm_back(mlp_ref[...], below_ref[0, 3:4, :], grad_stream)
        low_ref[...] = grad_mlp.astype(BF16)

    rows, columns = pair.shape
    return kernel_call(
        body,
        [shape(rows, columns, F32), shape(rows, columns, BF16)] + [shape(1, columns, F32)] * 2,
        (pair, other, stream, grad_middle, mlp_sum, gains, gains),
        {5: layer, 6: layer - 1},
    )


def back_to_input(pair, other, stream, grad_middle, gains, layer):
    def body(pair_ref, other_ref, stream_ref, grad_ref, gains_ref, out_ref):
        own = out_ref.shape[0]
        grad_normed = pair_ref[:own, :].astype(F32) + other_ref[own:, :].astype(F32)
        step, unused = norm_back(
            stream_ref[:own, :].astype(F32), gains_ref[0, 0:1, :], grad_normed
        )
        out_ref[...] = (grad_ref[:own, :] + step).astype(BF16)

    rows, columns = pair.shape
    return kernel_call(
        body,
        [shape(rows // 2, columns, BF16)],
        (pair, other, stream, grad_middle, gains),
        {4: layer},
    )[0]


def allowed_rows(down_ref, across_ref, start, count, window):
    seg_down = down_ref[start : start + count, 0:1]
    place_down = down_ref[start : start + count, 1:2]
    seg_across = across_ref[0:1, :]
    place_across = across_ref[1:2, :]
    allowed = (seg_down == seg_across) & (place_across <= place_down)
    if window < SEQ_LEN:
        allowed = allowed & (place_down - place_across < window)
    return allowed


def attention(own, received, weights, tables, layer, window):
    w_query, w_key, w_value, w_out, qk_gains = weights
    cosine, sine, down, across = tables
    half = own.shape[0]
    length = 2 * half
    head_width = w_key.shape[2]

    def body(
        own_ref, received_ref, wq_ref, wk_ref, wv_ref, wo_ref, gain_ref,
        cos_ref, sin_ref, down_ref, across_ref,
        kept_ref, sent_ref, qraw_ref, kraw_ref, q_ref, k_ref, v_ref, attended_ref, lse_ref,
    ):
        for part, source in ((0, own_ref), (1, received_ref)):
            rows = slice(part * half, (part + 1) * half)
            normed = source[...]
            cos_rows, sin_rows = cos_ref[rows, :], sin_ref[rows, :]
            key_raw = product(normed, wk_ref[0])
            kraw_ref[rows, :] = key_raw
            k_ref[rows, :] = rotate(
                norm_forward(key_raw, gain_ref[0, 1:2, :]), cos_rows, sin_rows
            ).astype(BF16)
            v_ref[rows, :] = product(normed, wv_ref[0]).astype(BF16)
            query_raw = product(normed, wq_ref[0])
            qraw_ref[rows, :] = query_raw
            q_ref[rows, :] = rotate(
                norm_forward(query_raw, gain_ref[0, 0:1, :]), cos_rows, sin_rows
            ).astype(BF16)
        for part, target in ((1, sent_ref), (0, kept_ref)):
            rows = slice(part * half, (part + 1) * half)
            scores = product_right(q_ref[rows, :], k_ref[...]) * score_scale
            allowed = allowed_rows(down_ref, across_ref, part * half, half, window)
            masked = jnp.where(allowed, scores, masked_fill)
            row_max = jnp.max(masked, axis=-1, keepdims=True)
            expo = jnp.where(allowed, jnp.exp(masked - row_max), 0.0)
            row_sum = jnp.sum(expo, axis=-1, keepdims=True)
            probability = (expo * (1.0 / row_sum)).astype(BF16)
            lse_ref[rows, :] = row_max + jnp.log(row_sum)
            attended = product(probability, v_ref[...]).astype(BF16)
            attended_ref[rows, :] = attended
            target[...] = product(attended, wo_ref[0]).astype(BF16)

    width = own.shape[1]
    return kernel_call(
        body,
        [shape(half, width, BF16)] * 2
        + [shape(length, head_width, F32)] * 2
        + [shape(length, head_width, BF16)] * 4
        + [shape(length, 1, F32)],
        (own, received, w_query, w_key, w_value, w_out, qk_gains, cosine, sine, down, across),
        {place: layer for place in (2, 3, 4, 5, 6)}, cost=FORWARD_COST)


def feed_forward(own, received, weights, layer):
    half, width = own.shape
    w_gate, w_up, w_down = weights
    hidden_width = w_gate.shape[2]
    length = 2 * half

    def body(own_ref, received_ref, wg_ref, wu_ref, wd_ref, kept_ref, sent_ref, g_ref, u_ref, h_ref):
        for part, source, target in ((1, received_ref, sent_ref), (0, own_ref, kept_ref)):
            rows = slice(part * half, (part + 1) * half)
            normed = source[...]
            gate = product(normed, wg_ref[0])
            up = product(normed, wu_ref[0])
            g_ref[rows, :] = gate
            u_ref[rows, :] = up
            bend = jnp.tanh(gelu_slope * (gate + gelu_cubic * (gate * gate * gate)))
            hidden = (gate * (0.5 * (1.0 + bend)) * up).astype(BF16)
            h_ref[rows, :] = hidden
            target[...] = product(hidden, wd_ref[0]).astype(BF16)

    return kernel_call(
        body,
        [shape(half, width, BF16)] * 2
        + [shape(length, hidden_width, F32)] * 2
        + [shape(length, hidden_width, BF16)],
        (own, received, w_gate, w_up, w_down),
        {2: layer, 3: layer, 4: layer}, cost=FORWARD_COST)


def feed_forward_back(own, received, weights, gate, up, layer):
    half, width = own.shape
    w_gate, w_up, w_down = weights
    hidden_width = w_gate.shape[2]
    length = 2 * half

    def body(
        own_ref, received_ref, wg_ref, wu_ref, wd_ref, g_ref, u_ref,
        kept_ref, sent_ref, gate_low_ref, up_low_ref,
    ):
        for part, source, target in ((1, received_ref, sent_ref), (0, own_ref, kept_ref)):
            rows = slice(part * half, (part + 1) * half)
            grad_hidden = product_right(source[...], wd_ref[0])
            gate_in = g_ref[rows, :]
            square = gate_in * gate_in
            bend = jnp.tanh(gelu_slope * gate_in * (1.0 + gelu_cubic * square))
            lift = 0.5 * (1.0 + bend)
            slope = lift + 0.5 * gate_in * (1.0 - bend * bend) * (
                gelu_slope * (1.0 + 3.0 * gelu_cubic * square)
            )
            gate_low = (grad_hidden * u_ref[rows, :] * slope).astype(BF16)
            up_low = (grad_hidden * (gate_in * lift)).astype(BF16)
            gate_low_ref[rows, :] = gate_low
            up_low_ref[rows, :] = up_low
            target[...] = (
                product_right(gate_low, wg_ref[0]) + product_right(up_low, wu_ref[0])
            ).astype(BF16)

    return kernel_call(
        body,
        [shape(half, width, BF16)] * 2 + [shape(length, hidden_width, BF16)] * 2,
        (own, received, w_gate, w_up, w_down, gate, up),
        {2: layer, 3: layer, 4: layer},
    )


def attention_back(own, received, weights, tables, saved, side, layer, window, first=()):
    w_query, w_key, w_value, w_out, qk_gains = weights
    cosine, sine, down, across = tables
    query_raw, key_raw, queries, key_rows, values, row_lse = saved
    half, width = own.shape
    length = 2 * half
    head_width = w_key.shape[2]

    def body(
        own_ref, received_ref, wq_ref, wk_ref, wv_ref, wo_ref, gain_ref,
        cos_ref, sin_ref, down_ref, across_ref,
        qraw_ref, kraw_ref, q_ref, k_ref, v_ref, lse_ref, side_ref,
        *rest,
    ):
        firsts, rest = rest[: len(first)], rest[len(first) :]
        kept_ref, sent_ref, gq_ref, mine_ref, theirs_ref, qgain_ref, kgain_ref = rest[:7]
        *gain0_refs, gk_ref, gv_ref = rest[7:]
        grad_keys = None
        grad_values = None
        query_gain = None
        for part, source in ((0, own_ref), (1, received_ref)):
            rows = slice(part * half, (part + 1) * half)
            grad_attended = product_right(source[...], wo_ref[0]).astype(BF16)
            queries_part = q_ref[rows, :]
            scores = product_right(queries_part, k_ref[...]) * score_scale
            allowed = allowed_rows(down_ref, across_ref, part * half, half, window)
            probability = jnp.where(allowed, jnp.exp(scores - lse_ref[rows, :]), 0.0)
            values_term = product_left(probability.astype(BF16), grad_attended)
            grad_prob = product_right(grad_attended, v_ref[...])
            inner_sum = jnp.sum(probability * grad_prob, axis=-1, keepdims=True)
            grad_scores = (probability * (grad_prob - inner_sum)).astype(BF16)
            keys_term = product_left(grad_scores, queries_part)
            grad_values = values_term if grad_values is None else grad_values + values_term
            grad_keys = keys_term if grad_keys is None else grad_keys + keys_term
            grad_queries = (product(grad_scores, k_ref[...]) * score_scale).astype(BF16)
            turned = rotate(grad_queries.astype(F32), cos_ref[rows, :], -sin_ref[rows, :])
            grad_raw, gain_term = norm_back(qraw_ref[rows, :], gain_ref[0, 0:1, :], turned)
            query_gain = gain_term if query_gain is None else query_gain + gain_term
            gq_ref[rows, :] = grad_raw.astype(BF16)
        qgain_ref[...] = query_gain
        grad_keys = (grad_keys * score_scale).astype(BF16)
        turned = rotate(grad_keys.astype(F32), cos_ref[...], -sin_ref[...])
        grad_raw, kgain_ref[...] = norm_back(kraw_ref[...], gain_ref[0, 1:2, :], turned)
        gk_ref[...] = grad_raw.astype(BF16)
        gv_ref[...] = grad_values.astype(BF16)

        @pl.when(side_ref[0] == 0)
        def keys_here():
            mine_ref[...] = gk_ref[...]
            theirs_ref[...] = gv_ref[...]

        @pl.when(side_ref[0] != 0)
        def values_here():
            mine_ref[...] = gv_ref[...]
            theirs_ref[...] = gk_ref[...]

        for part, target in ((1, sent_ref), (0, kept_ref)):
            rows = slice(part * half, (part + 1) * half)
            target[...] = (
                product_right(gq_ref[rows, :], wq_ref[0])
                + product_right(gk_ref[rows, :], wk_ref[0])
                + product_right(gv_ref[rows, :], wv_ref[0])
            ).astype(BF16)
        if first:
            low_ref, other_ref, norm_ref = firsts
            gain0_refs[0][...] = (
                jnp.sum(
                    kept_ref[...].astype(F32) * low_ref[...].astype(F32)
                    + sent_ref[...].astype(F32) * other_ref[...].astype(F32),
                    axis=0,
                    keepdims=True,
                )
                / norm_ref[0, 0:1, :]
            )

    fixed = {place: layer for place in (2, 3, 4, 5, 6)}
    if first:
        fixed[20] = layer
    return kernel_call(
        body,
        [shape(half, width, BF16)] * 2
        + [shape(length, head_width, BF16)] * 3
        + [shape(1, head_width, F32)] * 2
        + [shape(1, width, F32)] * (1 if first else 0),
        (
            own, received, w_query, w_key, w_value, w_out, qk_gains,
            cosine, sine, down, across, query_raw, key_raw, queries, key_rows, values, row_lse, side,
            *first,
        ),
        fixed,
        scratch=[pltpu.VMEM((length, head_width), BF16)] * 2,
    )


def slot_masks(bits):
    count = len(bits)
    return [
        sum(bit for place, bit in enumerate(bits) if slot >> (count - 1 - place) & 1)
        for slot in range(1 << count)
    ]


def gradient_blocks(factors, me, bits, gains=()):
    pieces = 1 << len(bits)
    masks = slot_masks(bits)
    sizes = [(l[0].shape[1] // pieces, r[0].shape[1] // LANES) for l, r in factors]
    rows = sum(tall * wide for tall, wide in sizes)
    if any(tall % 16 for tall, wide in sizes):
        chunks = me[0] ^ jnp.array(masks, jnp.int32)
        parts = []
        for (left, right), (tall, wide) in zip(factors, sizes):
            grad = product_left(jnp.concatenate(left), jnp.concatenate(right)).astype(BF16)
            cut = grad.reshape(pieces, tall, wide, LANES).transpose(0, 2, 1, 3)
            parts.append(cut.reshape(pieces, tall * wide, LANES))
        if gains:
            rows = [
                jnp.pad(row.reshape(pieces, 1, -1), ((0, 0), (0, 0), (0, LANES - row.shape[1] // pieces)))
                for row in gains
            ]
            block = jnp.concatenate(rows, axis=1)
            parts.append(
                jnp.pad(block, ((0, 0), (0, GAIN_ROWS - len(rows)), (0, 0))).astype(BF16)
            )
        blocks = jnp.take(jnp.concatenate(parts, axis=1), chunks, axis=0)
        return (blocks[: pieces // 2], blocks[pieces // 2 :])
    flat = []
    where = []
    for pair in factors:
        places = []
        for side in pair:
            places.append(list(range(len(flat), len(flat) + len(side))))
            flat.extend(side)
        where.append(places)

    def body(*refs):
        me_ref, inputs = refs[0], refs[1 : 1 + len(flat)]
        gain_refs = refs[1 + len(flat) : 1 + len(flat) + len(gains)]
        kept_ref, sent_ref, *scratch = refs[1 + len(flat) + len(gains) :]
        base = 0
        for (lefts, rights), (tall, wide), held in zip(where, sizes, scratch):
            def side(places):
                arrays = [inputs[place][...] for place in places]
                return arrays[0] if len(arrays) == 1 else jnp.concatenate(arrays, axis=0)

            held[...] = product_left(side(lefts), side(rights))
            for slot, mask in enumerate(masks):
                chunk = jnp.bitwise_xor(me_ref[0], mask)
                start = pl.multiple_of(chunk * tall, tall)
                target = kept_ref if slot < pieces // 2 else sent_ref
                block = held[pl.ds(start, tall), :].astype(BF16)
                for column in range(wide):
                    low = base + column * tall
                    target[slot % (pieces // 2), low : low + tall, :] = block[
                        :, column * LANES : (column + 1) * LANES
                    ]
            base += tall * wide
        if gains:
            table = scratch[-1]
            table[...] = jnp.zeros_like(table)
            for place, ref in enumerate(gain_refs):
                count = ref.shape[1] // pieces
                for chunk in range(pieces):
                    line = chunk * GAIN_ROWS + place
                    table[line : line + 1, :count] = ref[:, chunk * count : (chunk + 1) * count]
            for slot, mask in enumerate(masks):
                chunk = jnp.bitwise_xor(me_ref[0], mask)
                start = pl.multiple_of(chunk * GAIN_ROWS, GAIN_ROWS)
                target = kept_ref if slot < pieces // 2 else sent_ref
                target[slot % (pieces // 2), base : base + GAIN_ROWS, :] = table[
                    pl.ds(start, GAIN_ROWS), :
                ].astype(BF16)

    rows += GAIN_ROWS if gains else 0
    out = jax.ShapeDtypeStruct((pieces // 2, rows, LANES), BF16)
    args = (me, *flat, *gains)
    specs = [pl.BlockSpec(memory_space=pltpu.SMEM)] + [
        pl.BlockSpec(a.shape, lambda i: (0, 0)) for a in args[1:]
    ]
    return pl.pallas_call(
        body,
        grid=(1,),
        in_specs=specs,
        out_specs=[pl.BlockSpec(out.shape, lambda i: (0, 0, 0))] * 2,
        out_shape=[out, out],
        scratch_shapes=[
            pltpu.VMEM((tall * pieces, wide * LANES), F32) for tall, wide in sizes
        ]
        + [pltpu.VMEM((pieces * GAIN_ROWS, LANES), F32)] * (1 if gains else 0),
        compiler_params=pltpu.CompilerParams(vmem_limit_bytes=VMEM_BYTES),
        cost_estimate=pl.CostEstimate(flops=1, transcendentals=0, bytes_accessed=1),
    )(*args)


def after(gate, *values):
    return lax.optimization_barrier((gate,) + values)[1:]


class Halving:
    def __init__(self, terms, me, bits, gains=()):
        self.kept, sent = gradient_blocks(terms, me, bits, gains)
        self.bits = bits
        self.arrived = swap(sent, "dp", bits[0])

    def step(self, gate=None):
        if not self.bits:
            return
        kept, arrived = self.kept, self.arrived
        if gate is not None:
            kept, arrived = after(gate, kept, arrived)
        self.bits = self.bits[1:]
        if self.bits:
            middle = kept.shape[0] // 2
            sent = (kept[middle:].astype(F32) + arrived[middle:].astype(F32)).astype(BF16)
            self.arrived = swap(sent, "dp", self.bits[0])
            self.kept = kept[:middle].astype(F32) + arrived[:middle].astype(F32)
        else:
            self.kept = kept[0].astype(F32) + arrived[0].astype(F32)

    def finish(self):
        while self.bits:
            self.step()
        return self.kept


def assembled(sources, layout, sizes, exchanged, starts, shared_size, gains_at, gain_widths):
    sizes = sizes + [shared_size] * 2
    here, there, side = exchanged
    outs = [jax.ShapeDtypeStruct((2, tall, columns), F32) for tall, columns in sizes]
    outs += [
        jax.ShapeDtypeStruct((2, 4, gain_widths[0]), F32),
        jax.ShapeDtypeStruct((2, 2, gain_widths[1]), F32),
    ]

    if any(tall % 16 for tall, columns in sizes):

        def joined(array, start, tall, columns):
            return jnp.concatenate(
                [
                    array[start + place * tall : start + (place + 1) * tall]
                    for place in range(columns // LANES)
                ],
                axis=1,
            ).astype(F32)

        results = [
            jnp.stack([joined(sources[source], start, *size) for source, start in both])
            for both, size in zip(layout, sizes)
        ]
        for first, second in ((here, there), (there, here)):
            picked = jnp.where(side == 0, first, second)
            results.append(jnp.stack([joined(picked, start, *shared_size) for start in starts]))
        gains = here[gains_at : gains_at + GAIN_ROWS].astype(F32)
        gains = (gains + there[gains_at : gains_at + GAIN_ROWS].astype(F32))[:12]
        gains = gains.reshape(2, 6, LANES)
        return results + [gains[:, :4, : gain_widths[0]], gains[:, 4:, : gain_widths[1]]]

    def body(*refs):
        inputs = refs[: len(sources)]
        here_ref, there_ref, side_ref = refs[len(sources) : len(sources) + 3]
        *targets, norm_ref, qk_ref = refs[len(sources) + 3 :]

        def put(target, layer, source, start, tall, columns):
            for column in range(columns // LANES):
                low = start + column * tall
                target[layer, :, column * LANES : (column + 1) * LANES] = source[
                    low : low + tall, :
                ].astype(F32)

        for member, both in enumerate(layout):
            for layer, (source, start) in enumerate(both):
                put(targets[member], layer, inputs[source], start, *sizes[member])
        key_ref, value_ref = targets[-2:]

        @pl.when(side_ref[0] == 0)
        def keys_here():
            for layer, start in enumerate(starts):
                put(key_ref, layer, here_ref, start, *shared_size)
                put(value_ref, layer, there_ref, start, *shared_size)

        @pl.when(side_ref[0] != 0)
        def values_here():
            for layer, start in enumerate(starts):
                put(key_ref, layer, there_ref, start, *shared_size)
                put(value_ref, layer, here_ref, start, *shared_size)

        gains = here_ref[gains_at : gains_at + GAIN_ROWS, :].astype(F32)
        gains = gains + there_ref[gains_at : gains_at + GAIN_ROWS, :].astype(F32)
        for layer in range(2):
            norm_ref[layer] = gains[6 * layer : 6 * layer + 4, : gain_widths[0]]
            qk_ref[layer] = gains[6 * layer + 4 : 6 * layer + 6, : gain_widths[1]]

    return kernel_call(body, outs, (*sources, here, there, side))


def local(
    hidden_in,
    cotangent,
    segments,
    positions,
    w_query,
    w_key,
    w_value,
    w_out,
    w_gate,
    w_up,
    w_down,
    norm_gains,
    qk_gains,
):
    head_width = w_key.shape[2]
    windows = (WINDOW, SEQ_LEN)
    pieces = lax.axis_size("dp")
    quarter = lax.axis_index("tensor")
    me = lax.axis_index("dp").astype(jnp.int32).reshape(1)
    side = jnp.bitwise_and(quarter, 1).astype(jnp.int32).reshape(1)
    hidden_in, segments, positions, quarter, me, side = lax.optimization_barrier(
        (hidden_in, segments, positions, quarter, me, side)
    )
    bits = [1 << place for place in range(pieces.bit_length() - 1)]
    mlp1_bits = [bits[p] for p in [0, 1, 2]] + bits[3:] if len(bits) > 2 else bits
    attn1_bits = [bits[p] for p in [0, 1, 2]] + bits[3:] if len(bits) > 2 else bits
    mlp0_bits = [bits[p] for p in [0, 1, 2]] + bits[3:] if len(bits) > 2 else bits
    attn0_bits = [bits[p] for p in [1, 0, 2]] + bits[3:] if len(bits) > 2 else bits
    across, down = ordered_rows(segments, positions, quarter.reshape(1))
    attn_weights = (w_query, w_key, w_value, w_out, qk_gains)
    mlp_weights = (w_gate, w_up, w_down)
    tables = [angles(down, head_width, thetas[0]) + (down, across), None]

    beside = swap(hidden_in, "tensor", 2)
    (beside,) = after(tables[0], beside)
    stream, low = first_norm(hidden_in, beside, norm_gains, 0)
    saved = []
    for layer in range(2):
        received = swap(low, "tensor", 1)
        kept, sent, *kept_attn = attention(
            low, received, attn_weights, tables[layer], layer, windows[layer]
        )
        attn_in = (low, received)
        pair, other = summed_pair(kept, sent)
        if layer == 0:
            (rows,) = after(pair, down)
            tables[1] = angles(rows, head_width, thetas[1]) + (down, across)
            (other,) = after(tables[1], other)
        attn_sum, middle, low = after_attention(pair, other, stream, norm_gains, layer)
        received = swap(low, "tensor", 1)
        kept, sent, *kept_mlp = feed_forward(low, received, mlp_weights, layer)
        mlp_in = (low, received)
        pair, other = summed_pair(kept, sent)
        saved.append([attn_in, kept_attn, attn_sum, middle, mlp_in, kept_mlp, stream])
        if layer == 0:
            mlp_sum, stream, low = between_layers(pair, other, middle, norm_gains, layer)

    grad_stream = jnp.concatenate([cotangent, swap(cotangent, "tensor", 2)])
    output, low, gain3 = turn_around(pair, other, middle, grad_stream, norm_gains, 1)
    sums = {}
    gain_rows = [None, None]
    for layer in (1, 0):
        attn_in, kept_attn, attn_sum, middle, mlp_in, kept_mlp, stream = saved[layer]
        gate, up, hidden = kept_mlp
        query_raw, key_raw, queries, key_rows, values, attended, row_lse = kept_attn
        received = swap(low, "tensor", 1)
        kept, sent, gate_low, up_low = feed_forward_back(
            low, received, mlp_weights, gate, up, layer
        )
        mlp_out = (low, received)
        if layer == 0:
            sums["attn1"].step(gate_low)
            (kept,) = after(sums["attn1"].kept, kept)
        pair, other = summed_pair(kept, sent)
        gate_low, up_low = after(pair, gate_low, up_low)
        gate_term, up_term = (mlp_in, (gate_low,)), (mlp_in, (up_low,))
        down_term = ((hidden,), mlp_out)
        if layer == 1:
            sums["mlp1"] = Halving([gate_term, up_term, down_term], me, mlp1_bits)
            (other,) = after(sums["mlp1"].kept, other)
        else:
            sums["mlp0"] = Halving([gate_term, up_term, down_term], me, mlp0_bits)
            sums["mlp1"].step((sums["mlp0"].kept, other))
            (other,) = after([s.kept for s in sums.values()], other)
        grad_middle, low, gain1, gain2 = back_to_attention(
            pair, other, middle, attn_sum, grad_stream, norm_gains, layer
        )
        received = swap(low, "tensor", 1)
        kept, sent, grad_q, mine, theirs, gain_q, gain_k, *gain0 = attention_back(
            low,
            received,
            attn_weights,
            tables[layer],
            (query_raw, key_raw, queries, key_rows, values, row_lse),
            side,
            layer,
            windows[layer],
            () if layer else (*attn_in, norm_gains),
        )
        pair, other = summed_pair(kept, sent)
        theirs = swap(theirs, "tensor", 1)
        if layer == 1:
            grad_q, mine, theirs = after(pair, grad_q, mine, theirs)
        shared_term = (attn_in + attn_in[::-1], (mine, theirs))
        query_term, out_term = (attn_in, (grad_q,)), ((attended,), (low, received))
        gain_rows[layer] = [None, gain1 * 0.5, gain2 * 0.5, gain3 * 0.5, gain_q, gain_k]
        if layer == 1:
            sums["attn1"] = Halving([query_term, out_term, shared_term], me, attn1_bits)
            sums["mlp1"].step(sums["attn1"].kept)
            (other,) = after([s.kept for s in sums.values()], other)
            grad_stream, low, gain0, gain3 = back_between(
                pair, other, stream, grad_middle, mlp_sum, norm_gains, layer
            )
            gain_rows[1][0] = gain0 * 0.5
        else:
            gain_rows[0][0] = gain0[0]
            sums["attn0"] = Halving(
                [query_term, out_term, shared_term],
                me,
                attn0_bits,
                gain_rows[0] + gain_rows[1],
            )
            grad_input = back_to_input(pair, other, stream, grad_middle, norm_gains, layer)

    sums["attn1"].step(sums["attn0"].kept)
    sums["mlp1"].step(sums["attn1"].kept)
    sums["mlp0"].step(sums["attn0"].kept)
    sums["attn0"].step(sums["mlp0"].kept)
    sums["attn0"].step()
    sums["mlp0"].step(sums["attn0"].kept)
    sums["attn0"].finish()

    tall = {
        "q": w_query.shape[1] // pieces,
        "o": w_out.shape[1] // pieces,
        "g": w_gate.shape[1] // pieces,
        "d": w_down.shape[1] // pieces,
    }
    heads_rows = tall["q"] * head_width // LANES
    gate_rows = tall["g"] * w_gate.shape[2] // LANES
    both_rows = heads_rows + tall["o"] * w_out.shape[2] // LANES
    done = {name: halving.finish() for name, halving in sums.items()}
    low = jnp.concatenate([done["attn0"][both_rows:], done["attn1"][both_rows:]]).astype(BF16)
    here = (low.astype(F32) + swap(low, "tensor", 2).astype(F32)).astype(BF16)
    there = swap(here, "tensor", 1)
    first_rows = done["attn0"].shape[0] - both_rows
    *grads, grad_norm_gains, grad_qk_gains = assembled(
        [done[name] for name in ("attn0", "attn1", "mlp0", "mlp1")],
        [
            [(0, 0), (1, 0)],
            [(0, heads_rows), (1, heads_rows)],
            [(2, 0), (3, 0)],
            [(2, gate_rows), (3, gate_rows)],
            [(2, 2 * gate_rows), (3, 2 * gate_rows)],
        ],
        [(tall["q"], head_width), (tall["o"], w_out.shape[2])]
        + [(tall["g"], w_gate.shape[2])] * 2
        + [(tall["d"], w_down.shape[2])],
        (here, there, side),
        [0, first_rows],
        (tall["q"], head_width),
        first_rows - GAIN_ROWS,
        (norm_gains.shape[2] // pieces, head_width // pieces),
    )
    grad_query, grad_out, grad_gate, grad_up, grad_down, grad_key, grad_value = grads
    return (
        output,
        grad_input,
        grad_query,
        grad_key,
        grad_value,
        grad_out,
        grad_gate,
        grad_up,
        grad_down,
        grad_norm_gains,
        grad_qk_gains,
    )


def solution(mesh):
    return jax.shard_map(
        local,
        mesh=mesh,
        in_specs=(
            P(("dp", "tensor"), None),
            P(("dp", "tensor"), None),
            P("dp"),
            P("dp"),
            P(None, None, "tensor"),
            P(),
            P(),
            P(None, "tensor", None),
            P(None, None, "tensor"),
            P(None, None, "tensor"),
            P(None, "tensor", None),
            P(),
            P(),
        ),
        out_specs=(
            P(("dp", "tensor"), None),
            P(("dp", "tensor"), None),
            P(None, "dp", "tensor"),
            P(None, "dp", None),
            P(None, "dp", None),
            P(None, ("tensor", "dp"), None),
            P(None, "dp", "tensor"),
            P(None, "dp", "tensor"),
            P(None, ("tensor", "dp"), None),
            P(None, None, "dp"),
            P(None, None, "dp"),
        ),
        check_vma=False,
    )
```
